256 devices in a mesh: tm: 64 (over y, x_lo, z), space: 4 (over x_hi, core).
Axes of the slice: x: 4 (x_hi: 2, x_lo: 2; x = x_hi * 2 + x_lo), y: 4, z: 8, core: 2. Of those that a mesh axis runs over, the one named last changes fastest.
Arguments:
- end_state: float32 [64, 5, 64, 1024], P('tm', None, None, 'space'), may hold values from -6 to 6
- forcing: bfloat16 [64, 2, 5, 64, 1024], P('tm', None, None, None, 'space'), may hold values from -3 to 3
- jacobians: float32 [64, 3, 5, 5, 1024], P('tm', None, None, None, 'space'), may hold values from -2.7 to 2.7
- coarse_blocks: float32 [64, 5, 5, 1024], P('tm', None, None, 'space'), as said below
- neighbors: int32 [6, 1024], P(None, 'space'), may hold values from 0 to 511, as said below
- orientation: int32 [6, 1024], P(None, 'space'), may hold values from 0 to 7
- interfaces: int32 [2, 512], P(None, 'space'), may hold values from 0 to 255, as said below
Outputs:
- new_end: float32 [64, 5, 64, 1024], P('tm', None, None, 'space')
The draws below stay inside these ranges and needn't reach their ends.
Inputs may be any that keep to these rules, and one draw needn't show every extreme that they name: `neighbors`: entry [k, e] names the element across face k (-x, +x, -y, +y, -z, +z) of local element e of the same partition. Only -x faces of the partition's first layer hold 256 + s and only +x faces of its last layer hold 384 + s; s indexes row 1 of interfaces of the partition before, or row 0 of the partition after; y and z wrap inside a partition. `interfaces`: row 0 lists a partition's local elements whose -x face is its boundary, row 1 those whose +x face is, each ordered by position in y and z, so that slot s of row 1 faces slot s of row 0 of the next partition. `coarse_blocks`: one 5 x 5 block per interval and element.
All inputs are finite; a program needn't handle non-finite values.
Results may differ from the reference program's by a relative error of at most 0.0003.
Values sent between devices are 32-bit elements; how exact they have to be, the bound alone decides.
A program may use at most 64 MiB of HBM per device.

```python
import math
import jax
import jax.numpy as jnp
import numpy as np
from jax import lax

EX = 2
EY = 8
EZ = 16
WINDOW_COUNT = 64
SUBDOMAINS = 4
ELEMS = 256
SURFACE = 128


def cell_number(cell_x, cell_y, cell_z):
    return cell_x * (EY * EZ) + cell_y * EZ + cell_z


def layout_tables(key):
    neighbor_blocks = []
    interface_blocks = []
    for part_index in range(SUBDOMAINS):
        cell_of = jax.random.permutation(jax.random.fold_in(key, 1000 + part_index), ELEMS).astype(jnp.int32)
        local_of = jnp.argsort(cell_of).astype(jnp.int32)
        cell_x = cell_of // (EY * EZ)
        cell_y = cell_of // EZ % EY
        cell_z = cell_of % EZ
        slot_of = cell_y * EZ + cell_z
        minus_x = jnp.where(cell_x > 0, local_of[cell_number(jnp.maximum(cell_x - 1, 0), cell_y, cell_z)], ELEMS + slot_of)
        plus_x = jnp.where(cell_x < EX - 1, local_of[cell_number(jnp.minimum(cell_x + 1, EX - 1), cell_y, cell_z)], ELEMS + SURFACE + slot_of)
        minus_y = local_of[cell_number(cell_x, (cell_y + EY - 1) % EY, cell_z)]
        plus_y = local_of[cell_number(cell_x, (cell_y + 1) % EY, cell_z)]
        minus_z = local_of[cell_number(cell_x, cell_y, (cell_z + EZ - 1) % EZ)]
        plus_z = local_of[cell_number(cell_x, cell_y, (cell_z + 1) % EZ)]
        neighbor_blocks.append(jnp.stack([minus_x, plus_x, minus_y, plus_y, minus_z, plus_z]).astype(jnp.int32))
        slots = jnp.arange(SURFACE, dtype=jnp.int32)
        slot_y = slots // EZ
        slot_z = slots % EZ
        first_layer = local_of[cell_number(jnp.zeros_like(slots), slot_y, slot_z)]
        last_layer = local_of[cell_number(jnp.zeros_like(slots) + (EX - 1), slot_y, slot_z)]
        interface_blocks.append(jnp.stack([first_layer, last_layer]).astype(jnp.int32))
    return (jnp.concatenate(neighbor_blocks, axis=1), jnp.concatenate(interface_blocks, axis=1))


def draw_neighbors(key, part):
    return layout_tables(jax.random.fold_in(key, 77))[0]


def draw_interfaces(key, part):
    return layout_tables(jax.random.fold_in(key, 77))[1]


def draw_coarse_blocks(key, part):
    accumulated_grand = ELEMS * SUBDOMAINS
    reference_seed, noise_seed, spike_seed, imbalance_seed = jax.random.split(key, 4)
    nominal_speed = jnp.exp(jax.random.uniform(reference_seed, (1, 5, accumulated_grand), jnp.float32, math.log(0.05), math.log(20.0)))
    noise_magnitude = jnp.exp(jax.random.uniform(noise_seed, (WINDOW_COUNT, 5, accumulated_grand), jnp.float32, -0.7, 0.7))
    spike_magnitude = jnp.where(jax.random.uniform(spike_seed, (WINDOW_COUNT, 1, accumulated_grand), jnp.float32) < 0.06, 0.6, 1.0)
    damping_multiplier = jnp.exp(-3.0 * nominal_speed * noise_magnitude / WINDOW_COUNT) * spike_magnitude
    raw_skew = jax.random.uniform(imbalance_seed, (WINDOW_COUNT, 5, 5, accumulated_grand), jnp.float32, -1.0, 1.0) * (0.4 / math.sqrt(WINDOW_COUNT))
    skew_part = raw_skew - jnp.swapaxes(raw_skew, 1, 2)
    unit_blocks = jnp.eye(5, dtype=jnp.float32)[None, :, :, None]
    return (damping_multiplier[:, :, None, :] * (unit_blocks + skew_part)).astype(jnp.float32)


def set_ends(drawn, stream_key, smallest, largest):
    longest = drawn.shape.index(max(drawn.shape))
    spots = []
    for shift in (0, 1):
        where = [jax.random.randint(jax.random.fold_in(stream_key, axis), (), 0, length) for axis, length in enumerate(drawn.shape)]
        where[longest] = (where[longest] + shift) % drawn.shape[longest]
        spots.append(tuple(where))
    return drawn.at[spots[0]].set(smallest).at[spots[1]].set(largest)


def shard_levels(stream_key, dims, cuts, least, top_value):
    factor_of = 1.0
    for dim, shards_of in cuts:
        draws = jax.random.uniform(jax.random.fold_in(jax.random.fold_in(stream_key, 6), dim), (shards_of,), jnp.float32, least / len(cuts), top_value / len(cuts))
        factor_of = factor_of * jnp.repeat(jnp.exp(draws), dims[dim] // shards_of).reshape((-1,) + (1,) * (len(dims) - 1 - dim))
    return factor_of


def bell_draw(stream_key, dims, spread, most, pieces=(), kind=jnp.bfloat16):
    values = spread * jax.random.normal(stream_key, dims, jnp.float32)
    if pieces:
        values = values * shard_levels(stream_key, dims, pieces, -0.22, 0.18)
    return jnp.clip(values, -most, most).astype(kind)


def setup_inputs(seed: int = 0) -> dict:
    streams_of = jax.random.split(jax.random.key(seed), 8)
    end_state = bell_draw(streams_of[0], (WINDOW_COUNT, 5, 64, ELEMS * SUBDOMAINS), 1.0, 6.0, ((0, 64), (3, 4)), jnp.float32)
    forcing = bell_draw(streams_of[1], (WINDOW_COUNT, 2, 5, 64, ELEMS * SUBDOMAINS), 0.5, 3.0, ((0, 64), (4, 4)))
    jacobians = bell_draw(streams_of[2], (WINDOW_COUNT, 3, 5, 5, ELEMS * SUBDOMAINS), 0.45, 2.7, ((0, 64), (4, 4)), jnp.float32)
    coarse_blocks = draw_coarse_blocks(jax.random.fold_in(streams_of[7], 71), 0)
    neighbors = draw_neighbors(jax.random.fold_in(streams_of[7], 71), 0)
    orientation = set_ends(jax.random.randint(streams_of[5], (6, ELEMS * SUBDOMAINS), 0, 8), jax.random.fold_in(streams_of[5], 1), 0, 7).astype(jnp.int32)
    interfaces = draw_interfaces(jax.random.fold_in(streams_of[7], 71), 0)
    return {"end_state": end_state, "forcing": forcing, "jacobians": jacobians, "coarse_blocks": coarse_blocks, "neighbors": neighbors, "orientation": orientation, "interfaces": interfaces}


highest = lax.Precision.HIGHEST
step_size = 0.02
penalty = 0.5
lift_scale = 6.0

def tables():
    gll_nodes = np.array([-1.0, -math.sqrt(0.2), math.sqrt(0.2), 1.0])
    bary_weights = np.array([1.0 / np.prod([gll_nodes[j] - gll_nodes[k] for k in range(4) if k != j]) for j in range(4)])
    derivative = np.zeros((4, 4))
    for i in range(4):
        for j in range(4):
            if i != j:
                derivative[i, j] = bary_weights[j] / bary_weights[i] / (gll_nodes[i] - gll_nodes[j])
        derivative[i, i] = -derivative[i].sum()
    identity = np.eye(4)
    derivatives = np.stack([np.kron(np.kron(derivative, identity), identity), np.kron(np.kron(identity, derivative), identity), np.kron(np.kron(identity, identity), derivative)])
    weights = np.array([1.0, 5.0, 5.0, 1.0]) / 6.0
    cube_weights = (weights[:, None, None] * weights[None, :, None] * weights[None, None, :]).reshape(64) / 8.0
    node_grid = np.arange(64).reshape(4, 4, 4)
    face_nodes = np.stack([node_grid[0].reshape(16), node_grid[3].reshape(16), node_grid[:, 0].reshape(16), node_grid[:, 3].reshape(16), node_grid[:, :, 0].reshape(16), node_grid[:, :, 3].reshape(16)])
    face_grid = np.arange(16).reshape(4, 4)
    orientations = []
    for symmetry in range(8):
        arranged = face_grid
        if symmetry & 4:
            arranged = arranged.T
        if symmetry & 2:
            arranged = arranged[::-1]
        if symmetry & 1:
            arranged = arranged[:, ::-1]
        orientations.append(arranged.reshape(16))
    orientations = np.stack(orientations)
    lift_maps = np.zeros((6, 64, 16))
    for k in range(6):
        lift_maps[k, face_nodes[k], np.arange(16)] = lift_scale
    return (jnp.asarray(derivatives, jnp.float32), jnp.asarray(cube_weights, jnp.float32), face_nodes, orientations, jnp.asarray(lift_maps, jnp.float32))

def mix_fields(blocks, values):
    result = blocks[0][:, None] * values[0][None]
    for source in range(1, blocks.shape[0]):
        result = result + blocks[source][:, None] * values[source][None]
    return result

def reorient(fetched, orient_codes, orientations):
    result = jnp.zeros_like(fetched)
    for symmetry in range(8):
        result = result + jnp.where(orient_codes[None, None] == symmetry, fetched[:, orientations[symmetry]], 0.0)
    return result

def pick_along(values, indices):
    full_index = jnp.broadcast_to(indices[None, None], values.shape[:2] + indices.shape)
    return jnp.take_along_axis(values, full_index, axis=3)

def adjoint_step(adjoint, jacobian, forcing, neighbor_table, orient_table, interface_table, statics):
    derivatives, cube_weights, face_nodes, orientations, lift_maps = statics
    traces = [adjoint[:, face_nodes[k]] for k in range(6)]
    left_part = pick_along(traces[0], interface_table[0])
    right_part = pick_along(traces[1], interface_table[1])
    from_left = jnp.roll(right_part, 1, axis=2)
    from_right = jnp.roll(left_part, -1, axis=2)
    volume = jnp.zeros_like(adjoint)
    for axis_num in range(3):
        mixed_terms = mix_fields(jacobian[axis_num], adjoint)
        volume = volume + jnp.einsum('ji,fjpe->fipe', derivatives[axis_num], mixed_terms, precision=highest)
    for k in range(6):
        across = jnp.concatenate([traces[k ^ 1], from_left, from_right], axis=3)
        fetched = pick_along(across, neighbor_table[k])
        aligned = reorient(fetched, orient_table[k], orientations)
        trace_jump = aligned - traces[k]
        normal_sign = 0.5 if k % 2 == 1 else -0.5
        face_flux = normal_sign * mix_fields(jacobian[k // 2], trace_jump) + penalty * trace_jump
        volume = volume + jnp.einsum('ij,fjpe->fipe', lift_maps[k], face_flux, precision=highest)
    return adjoint + step_size * volume + forcing.astype(jnp.float32)

def apply_block(coarse_map, vector):
    return lax.optimization_barrier(jnp.sum(coarse_map * vector[None], axis=1))

def reference(end_state, forcing, jacobians, coarse_blocks, neighbors, orientation, interfaces):
    statics = tables()
    cube_weights = statics[1]
    part_count = SUBDOMAINS
    local_count = ELEMS
    neighbor_table = neighbors.reshape(6, part_count, local_count)
    orient_table = orientation.reshape(6, part_count, local_count)
    interface_table = interfaces.reshape(2, part_count, SURFACE)

    def relax(interval_args):
        adjoint, interval_forcing, interval_jac = interval_args
        adjoint = adjoint.reshape(5, 64, part_count, local_count)
        interval_jac = interval_jac.reshape(3, 5, 5, part_count, local_count)
        interval_forcing = interval_forcing.reshape(2, 5, 64, part_count, local_count)
        adjoint = adjoint_step(adjoint, interval_jac, interval_forcing[1], neighbor_table, orient_table, interface_table, statics)
        adjoint = adjoint_step(adjoint, interval_jac, interval_forcing[0], neighbor_table, orient_table, interface_table, statics)
        return adjoint.reshape(5, 64, part_count * local_count)
    starts = lax.map(relax, (end_state, forcing, jacobians))
    residual = jnp.roll(starts, 1, axis=0) - end_state
    coarse_residual = jnp.einsum('kfie,i->kfe', residual, cube_weights, precision=highest)

    def chain(earlier_value, interval_args):
        coarse_map, coarse_term = interval_args
        current = coarse_term + apply_block(coarse_map, earlier_value)
        return (current, current)
    zero_vector = jnp.zeros_like(coarse_residual[0])
    final_value, corrections = lax.scan(chain, zero_vector, (coarse_blocks, coarse_residual))
    return end_state + residual + corrections[:, :, None, :]
```

```python
import functools
import math

import jax
import jax.numpy as jnp
import ml_dtypes
import numpy as np
from jax import lax
from jax.experimental import pallas as pl
from jax.experimental.pallas import tpu as pltpu
from jax.sharding import PartitionSpec as P

MESH = pl.DeviceIdType.MESH
FIELDS = 5
NODES = 64
ROWS = FIELDS * NODES
ELEMS = 256
SURFACE = 128
STEP = 0.02
LIFT = 3.0
bf16 = jnp.bfloat16
f32 = jnp.float32


def tables():
    x = np.array([-1.0, -math.sqrt(0.2), math.sqrt(0.2), 1.0])
    bary = np.array([1.0 / np.prod([x[j] - x[k] for k in range(4) if k != j]) for j in range(4)])
    d1 = np.zeros((4, 4))
    for i in range(4):
        for j in range(4):
            if i != j:
                d1[i, j] = bary[j] / bary[i] / (x[i] - x[j])
        d1[i, i] = -d1[i].sum()
    eye = np.eye(4)
    derivs = [
        np.kron(np.kron(d1, eye), eye),
        np.kron(np.kron(eye, d1), eye),
        np.kron(np.kron(eye, eye), d1),
    ]
    w1 = np.array([1.0, 5.0, 5.0, 1.0]) / 6.0
    weights = (w1[:, None, None] * w1[None, :, None] * w1[None, None, :]).reshape(64) / 8.0
    n = np.arange(64)
    coords = [n // 16, n // 4 % 4, n % 4]
    blocks = []
    faces = np.zeros(64)
    for d in range(3):
        low, high = coords[d] == 0, coords[d] == 3
        faces += low.astype(float) + high.astype(float)
        blocks.append(STEP * (derivs[d].T + LIFT * np.diag(low.astype(float) - high.astype(float))))
    full = np.concatenate(blocks, axis=0)
    high_part = full.astype(ml_dtypes.bfloat16)
    low_part = (full - high_part.astype(np.float64)).astype(ml_dtypes.bfloat16)
    deriv = np.concatenate([high_part, high_part, low_part], axis=1)
    signs = [np.where(coords[d] == 0, -1.0, 1.0) for d in range(3)]
    own = 1.0 - STEP * LIFT * faces
    pattern = np.stack([weights, own] + signs).astype(np.float32)
    pattern = np.repeat(pattern.reshape(5 * 64, 1), 128, axis=1)
    return deriv, pattern


def face_node(k, p, q):
    if k < 2:
        return 48 * (k & 1) + 4 * p + q
    if k < 4:
        return 16 * p + 12 * (k & 1) + q
    return 16 * p + 4 * q + 3 * (k & 1)


def split(value):
    high = value.astype(bf16)
    low = (value - high.astype(f32)).astype(bf16)
    return jnp.concatenate([high, low], axis=0)


def gathered(both, chosen):
    out = jnp.dot(both, chosen, preferred_element_type=f32)
    half = out.shape[0] // 2
    return out[:half] + out[half:]


def one_hot(index_row, start, count):
    rows = lax.broadcasted_iota(jnp.int32, (count, index_row.shape[1]), 0) + start
    return jnp.where(rows == index_row, 1.0, 0.0).astype(bf16)


def wide(ref, *index):
    return jnp.concatenate([ref[(half, *index, slice(None))] for half in range(2)], axis=1)


def store_wide(ref, index, value):
    for half in range(2):
        ref[half, index, :] = value[:, 128 * half : 128 * half + 128]


def matvec(block, vector):
    total = wide(block, pl.ds(0, 5, stride=5)) * vector[0:1, :]
    for g in range(1, 5):
        total = total + wide(block, pl.ds(g, 5, stride=5)) * vector[g : g + 1, :]
    return total


def kernel(
    windows, parts, near, far,
    state_hbm, forcing_hbm, jac_hbm, coarse_hbm, neigh_hbm, orient_hbm, inter_hbm, deriv_hbm, pat_hbm,
    out_hbm,
    state, forcing, jac, coarse, neigh, orient, inter, deriv, pat,
    hot, hot_left, hot_right, hot_inter,
    fetched, lifted, terms, middle, start, shifted,
    halo_out, halo_in,
    blocks, products, ends, ends_next, coarse_out, coarse_in, window_out, window_in, result,
    in_sem, out_sem, halo_sem, block_sem, product_sem, end_sem, coarse_sem, window_sem, bulk_sem,
):
    tm = lax.axis_index("tm")
    space = lax.axis_index("space")

    def at_tm(distance):
        return {"tm": lax.rem(tm + (distance + windows), windows)}

    def at_space(distance):
        return {"space": lax.rem(space + (distance + parts), parts)}

    def send(src, dst, sems, index, target):
        copy = pltpu.make_async_remote_copy(
            src_ref=src, dst_ref=dst, send_sem=sems.at[0, index], recv_sem=sems.at[1, index],
            device_id=target, device_id_type=MESH,
        )
        copy.start()
        return copy

    loads = []
    for number, (src, dst) in enumerate([
        (inter_hbm, inter), (state_hbm, state), (neigh_hbm, neigh), (coarse_hbm, coarse),
        (orient_hbm, orient), (deriv_hbm, deriv), (pat_hbm, pat), (jac_hbm, jac), (forcing_hbm, forcing),
    ]):
        if dst is state:
            pair = [(src.at[:, 128 * half : 128 * half + 128], dst.at[half], 9 * half + number) for half in range(2)]
        else:
            pair = [(src, dst, number)]
        loads.append([pltpu.make_async_copy(a, b, in_sem.at[c]) for a, b, c in pair])
        for load in loads[-1]:
            load.start()

    def arrive(number):
        for load in loads[number]:
            load.wait()

    sources = sorted(set(range(1, near + 1)) | {near * m for m in range(1, far)} | {windows - 1})
    barrier = pltpu.get_barrier_semaphore()
    for distance in (1, -1):
        pl.semaphore_signal(barrier, inc=1, device_id=at_space(distance), device_id_type=MESH)
    for distance in sources:
        pl.semaphore_signal(barrier, inc=1, device_id=at_tm(-distance), device_id_type=MESH)

    lifted[...] = jnp.zeros_like(lifted)
    arrive(0)
    for side in range(2):
        hot_inter[side] = one_hot(inter[side : side + 1, :], 0, ELEMS)
    arrive(1)

    def trace_x(values, low):
        return jnp.concatenate([wide(values, slice(64 * f + low, 64 * f + low + 16)) for f in range(FIELDS)], axis=0)

    def halo_start(turn, values):
        right = split(trace_x(values, 48))
        left = split(trace_x(values, 0))
        halo_out[turn, 0] = gathered(right, hot_inter[1])
        halo_out[turn, 1] = gathered(left, hot_inter[0])
        return right, left

    def halo_send(turn):
        return [
            send(halo_out.at[turn, 0], halo_in.at[turn, 0], halo_sem, 2 * turn, at_space(1)),
            send(halo_out.at[turn, 1], halo_in.at[turn, 1], halo_sem, 2 * turn + 1, at_space(-1)),
        ]

    def local_part(values, right, left):
        store_wide(fetched, pl.ds(0, 80), gathered(right, hot[0]))
        store_wide(fetched, pl.ds(160, 80), gathered(left, hot[1]))
        for k in (2, 3):
            low = 8 if k == 2 else 0
            starts = [64 * f + 16 * a + low for f in range(FIELDS) for a in range(4)]
            rows = [wide(values, slice(first, first + 8)) for first in starts]
            store_wide(fetched, pl.ds(160 * k, 160), gathered(split(jnp.concatenate(rows, axis=0)), hot[k]))
        for k in (4, 5):
            low = 3 if k == 4 else 0
            rows = wide(values, pl.ds(low, 80, stride=4))
            store_wide(fetched, pl.ds(160 * k, 80), gathered(split(rows), hot[k]))
        for h in range(FIELDS):
            both = split(wide(values, slice(64 * h, 64 * h + 64)))
            stacked = jnp.concatenate([both, both[:64]], axis=0)
            terms[192 * h : 192 * h + 192, :] = jnp.dot(deriv[...], stacked, preferred_element_type=f32)

    def align(k):
        for half in range(2):
            code = orient[k : k + 1, 128 * half : 128 * half + 128]
            swap, flip_p, flip_q = [jnp.broadcast_to(code & bit, (FIELDS, 128)) != 0 for bit in (4, 2, 1)]
            grid = [[None] * 4 for _ in range(4)]
            for p in range(4):
                for q in range(4):
                    if k in (2, 3):
                        first, stride = 8 * p + (4 if k == 2 else 0) + q, 32
                    else:
                        first, stride = 4 * p + q, 16
                    grid[p][q] = fetched[half, pl.ds(160 * k + first, FIELDS, stride=stride), :]
            grid = [[grid[p][q] if p == q else jnp.where(swap, grid[q][p], grid[p][q]) for q in range(4)] for p in range(4)]
            grid = [[jnp.where(flip_p, grid[3 - p][q], grid[p][q]) for q in range(4)] for p in range(4)]
            grid = [[jnp.where(flip_q, grid[p][3 - q], grid[p][q]) for q in range(4)] for p in range(4)]
            for p in range(4):
                for q in range(4):
                    row = (k // 2 * 64 + face_node(k, p, q)) * 8
                    lifted[half, row : row + FIELDS, :] = (STEP * LIFT) * grid[p][q]

    def halo_part(turn):
        for side, chosen in enumerate((hot_left, hot_right)):
            rows = pl.ds(160 * side, 80)
            total = wide(fetched, rows) + gathered(split(halo_in[turn, side]), chosen[...])
            store_wide(fetched, rows, total)

    def mix(values, source, target):
        for group in range(2):
            low = 32 * group
            for half in range(2):
                lanes = slice(128 * half, 128 * half + 128)
                own = pat[64 + low : 96 + low, :]
                totals = [
                    own * values[half, 64 * f + low : 64 * f + low + 32, :]
                    + forcing[source, 64 * f + low : 64 * f + low + 32, lanes].astype(f32)
                    for f in range(FIELDS)
                ]
                for d in range(3):
                    sign = pat[128 + 64 * d + low : 160 + 64 * d + low, :]
                    for h in range(FIELDS):
                        face = lifted[half, pl.ds((64 * d + low) * 8 + h, 32, stride=8), :]
                        base = 192 * h + 64 * d + low
                        term = terms[base : base + 32, lanes] + sign * face
                        totals[h] = totals[h] + face
                        for f in range(FIELDS):
                            totals[f] = totals[f] + jac[5 * d + h, f : f + 1, lanes] * term
                for f in range(FIELDS):
                    target[half, 64 * f + low : 64 * f + low + 32, :] = totals[f]

    def node_sum(values):
        sums = []
        for f in range(FIELDS):
            halves = [
                jnp.sum(pat[0:64, :] * values[half, 64 * f : 64 * f + 64, :], axis=0, keepdims=True)
                for half in range(2)
            ]
            sums.append(jnp.concatenate(halves, axis=1))
        return jnp.concatenate(sums, axis=0)

    copies = []
    right, left = halo_start(0, state)
    pl.semaphore_wait(barrier, len(sources) + 2)
    halo = halo_send(0)
    arrive(3)
    keep = jnp.where(tm == 0, 0.0, 1.0)
    for f in range(FIELDS):
        store_wide(blocks.at[0], pl.ds(5 * f, 5), coarse[f] * keep)
    for m in range(1, near):
        copies.append(send(blocks.at[0], blocks.at[m], block_sem, m, at_tm(m)))
    arrive(6)
    ends[...] = node_sum(state)
    end_copy = send(ends, ends_next, end_sem, 0, at_tm(-1))
    arrive(2)
    for k in range(6):
        hot[k] = one_hot(neigh[k : k + 1, :], 0, ELEMS)
    hot_left[...] = one_hot(neigh[0:1, :], ELEMS, SURFACE)
    hot_right[...] = one_hot(neigh[1:2, :], ELEMS + SURFACE, SURFACE)
    arrive(5)
    local_part(state, right, left)
    arrive(4)
    for k in range(2, 6):
        align(k)
    for copy in halo:
        copy.wait()
    halo_part(0)
    align(0)
    align(1)
    arrive(7)
    arrive(8)
    mix(state, 1, middle)

    right, left = halo_start(1, middle)
    halo = halo_send(1)
    local_part(middle, right, left)
    for k in range(2, 6):
        align(k)
    for copy in copies:
        copy.wait()
    columns = [wide(blocks.at[near - 1], pl.ds(g, 5, stride=5)) for g in range(5)]
    for m in range(near - 2, -1, -1):
        columns = [matvec(blocks.at[m], column) for column in columns]
    for g in range(5):
        store_wide(products.at[0], pl.ds(g, 5, stride=5), columns[g])
    copies = [send(products.at[0], products.at[m], product_sem, m, at_tm(near * m)) for m in range(1, far - 1)]
    for copy in halo:
        copy.wait()
    halo_part(1)
    align(0)
    align(1)
    mix(middle, 0, start)

    end_copy.wait()
    coarse_out[...] = node_sum(start) - ends_next[...]
    rounds = [send(coarse_out, coarse_in.at[m], coarse_sem, m, at_tm(m + 1)) for m in range(near)]
    bulk = [
        send(start.at[:, pl.ds(64 * f, 64)], shifted.at[:, pl.ds(64 * f, 64)], bulk_sem, f, at_tm(1))
        for f in range(FIELDS)
    ]
    for copy in rounds:
        copy.wait()
    vector = coarse_in[near - 1]
    for m in range(near - 2, -1, -1):
        vector = coarse_in[m] + matvec(blocks.at[m], vector)
    window_out[...] = vector
    rounds = [send(window_out, window_in.at[m], window_sem, m, at_tm(near * m)) for m in range(1, far)]
    for copy in copies:
        copy.wait()
    for copy in rounds:
        copy.wait()
    vector = window_in[far - 1]
    for m in range(far - 2, 0, -1):
        vector = window_in[m] + matvec(products.at[m], vector)
    vector = window_out[...] + matvec(products.at[0], vector)
    outs = []
    for f in range(FIELDS):
        bulk[f].wait()
        rows = pl.ds(64 * f, 64)
        result[rows, :] = wide(shifted, rows) + vector[f : f + 1, :]
        copy = pltpu.make_async_copy(result.at[rows], out_hbm.at[rows], out_sem.at[f])
        copy.start()
        outs.append(copy)
    for copy in outs:
        copy.wait()


def solution(mesh):
    windows, parts = mesh.shape["tm"], mesh.shape["space"]
    near = 2 ** ((windows.bit_length() - 1) // 2)
    far = windows // near
    deriv, pattern = tables()
    dma = pltpu.SemaphoreType.DMA

    def per_device(end_state, forcing, jacobians, coarse_blocks, neighbors, orientation, interfaces):
        operands = (
            end_state.reshape(ROWS, ELEMS),
            forcing.reshape(2, ROWS, ELEMS),
            jacobians.reshape(15, 5, ELEMS),
            coarse_blocks.reshape(5, 5, ELEMS),
            neighbors,
            orientation,
            interfaces,
            jnp.asarray(deriv, bf16),
            jnp.asarray(pattern, f32),
        )
        out = pl.pallas_call(
            functools.partial(kernel, windows, parts, near, far),
            out_shape=jax.ShapeDtypeStruct((ROWS, ELEMS), f32),
            in_specs=[pl.BlockSpec(memory_space=pl.ANY)] * len(operands),
            out_specs=pl.BlockSpec(memory_space=pl.ANY),
            scratch_shapes=[pltpu.VMEM((2, ROWS, 128), f32)]
            + [pltpu.VMEM(x.shape, x.dtype) for x in operands[1:]]
            + [
                pltpu.VMEM((6, ELEMS, ELEMS), bf16),
                pltpu.VMEM((SURFACE, ELEMS), bf16),
                pltpu.VMEM((SURFACE, ELEMS), bf16),
                pltpu.VMEM((2, ELEMS, SURFACE), bf16),
                pltpu.VMEM((2, 6 * 160, 128), f32),
                pltpu.VMEM((2, 3 * 64 * 8, 128), f32),
                pltpu.VMEM((15 * 64, ELEMS), f32),
                pltpu.VMEM((2, ROWS, 128), f32),
                pltpu.VMEM((2, ROWS, 128), f32),
                pltpu.VMEM((2, ROWS, 128), f32),
                pltpu.VMEM((2, 2, 80, SURFACE), f32),
                pltpu.VMEM((2, 2, 80, SURFACE), f32),
                pltpu.VMEM((near, 2, 25, 128), f32),
                pltpu.VMEM((max(far - 1, 1), 2, 25, 128), f32),
                pltpu.VMEM((5, ELEMS), f32),
                pltpu.VMEM((5, ELEMS), f32),
                pltpu.VMEM((5, ELEMS), f32),
                pltpu.VMEM((near, 5, ELEMS), f32),
                pltpu.VMEM((5, ELEMS), f32),
                pltpu.VMEM((far, 5, ELEMS), f32),
                pltpu.VMEM((ROWS, ELEMS), f32),
                dma((18,)),
                dma((5,)),
                dma((2, 4)),
                dma((2, near)),
                dma((2, far)),
                dma((2, 1)),
                dma((2, near)),
                dma((2, far)),
                dma((2, 5)),
            ],
            compiler_params=pltpu.CompilerParams(
                collective_id=0, has_side_effects=True, vmem_limit_bytes=32 * 2**20
            ),
        )(*operands)
        return out.reshape(1, FIELDS, NODES, ELEMS)

    in_specs = (
        P("tm", None, None, "space"),
        P("tm", None, None, None, "space"),
        P("tm", None, None, None, "space"),
        P("tm", None, None, "space"),
        P(None, "space"),
        P(None, "space"),
        P(None, "space"),
    )
    out_specs = P("tm", None, None, "space")
    return jax.shard_map(per_device, mesh=mesh, in_specs=in_specs, out_specs=out_specs, check_vma=False)
```

```python
import functools
import math

import jax
import jax.numpy as jnp
import ml_dtypes
import numpy as np
from jax import lax
from jax.experimental import pallas as pl
from jax.experimental.pallas import tpu as pltpu
from jax.sharding import PartitionSpec as P

MESH = pl.DeviceIdType.MESH
FIELDS = 5
NODES = 64
ROWS = FIELDS * NODES
ELEMS = 256
SURFACE = 128
STEP = 0.02
LIFT = 3.0
EARLY = 2
bf16 = jnp.bfloat16
f32 = jnp.float32


def tables():
    x = np.array([-1.0, -math.sqrt(0.2), math.sqrt(0.2), 1.0])
    bary = np.array([1.0 / np.prod([x[j] - x[k] for k in range(4) if k != j]) for j in range(4)])
    d1 = np.zeros((4, 4))
    for i in range(4):
        for j in range(4):
            if i != j:
                d1[i, j] = bary[j] / bary[i] / (x[i] - x[j])
        d1[i, i] = -d1[i].sum()
    eye = np.eye(4)
    derivs = [
        np.kron(np.kron(d1, eye), eye),
        np.kron(np.kron(eye, d1), eye),
        np.kron(np.kron(eye, eye), d1),
    ]
    w1 = np.array([1.0, 5.0, 5.0, 1.0]) / 6.0
    weights = (w1[:, None, None] * w1[None, :, None] * w1[None, None, :]).reshape(64) / 8.0
    n = np.arange(64)
    coords = [n // 16, n // 4 % 4, n % 4]
    blocks = []
    faces = np.zeros(64)
    for d in range(3):
        low, high = coords[d] == 0, coords[d] == 3
        faces += low.astype(float) + high.astype(float)
        blocks.append(STEP * (derivs[d].T + LIFT * np.diag(low.astype(float) - high.astype(float))))
    full = np.concatenate(blocks, axis=0)
    high_part = full.astype(ml_dtypes.bfloat16)
    low_part = (full - high_part.astype(np.float64)).astype(ml_dtypes.bfloat16)
    deriv = np.concatenate([high_part, high_part, low_part], axis=1)
    signs = [np.where(coords[d] == 0, -1.0, 1.0) for d in range(3)]
    own = 1.0 - STEP * LIFT * faces
    pattern = np.stack([weights, own] + signs).astype(np.float32)
    pattern = np.repeat(pattern.reshape(5 * 64, 1), 128, axis=1)
    return deriv, pattern


def face_node(k, p, q):
    if k < 2:
        return 48 * (k & 1) + 4 * p + q
    if k < 4:
        return 16 * p + 12 * (k & 1) + q
    return 16 * p + 4 * q + 3 * (k & 1)


def split(value):
    high = value.astype(bf16)
    low = (value - high.astype(f32)).astype(bf16)
    return jnp.concatenate([high, low], axis=0)


def gathered(both, chosen):
    out = jnp.dot(both, chosen, preferred_element_type=f32)
    half = out.shape[0] // 2
    return out[:half] + out[half:]


def one_hot(index_row, start, count):
    rows = lax.broadcasted_iota(jnp.int32, (count, index_row.shape[1]), 0) + start
    return jnp.where(rows == index_row, 1.0, 0.0).astype(bf16)


def wide(ref, *index):
    return jnp.concatenate([ref[(half, *index, slice(None))] for half in range(2)], axis=1)


def store_wide(ref, index, value):
    for half in range(2):
        ref[half, index, :] = value[:, 128 * half : 128 * half + 128]


def column(block, g):
    return jnp.concatenate([block[pl.ds(2 * g + half, 5, stride=10), :] for half in range(2)], axis=1)


def matvec(block, vector):
    total = column(block, 0) * vector[0:1, :]
    for g in range(1, 5):
        total = total + column(block, g) * vector[g : g + 1, :]
    return total


def kernel(
    windows, parts, near, far,
    state_hbm, forcing_hbm, jac_hbm, coarse_hbm, neigh_hbm, orient_hbm, inter_hbm, deriv_hbm, pat_hbm,
    shifted, correction,
    state, forcing, jac, coarse, neigh, orient, inter, deriv, pat,
    hot, hot_left, hot_right, hot_inter,
    fetched, lifted, terms, middle, start,
    halo_out, halo_in,
    blocks, products, ends, ends_next, coarse_out, coarse_in, window_out, window_in,
    in_sem, halo_sem, block_sem, product_sem, end_sem, coarse_sem, window_sem, bulk_sem,
):
    tm = lax.axis_index("tm")
    space = lax.axis_index("space")

    def at_tm(distance):
        return {"tm": lax.rem(tm + (distance + windows), windows)}

    def at_space(distance):
        return {"space": lax.rem(space + (distance + parts), parts)}

    def send(src, dst, sems, index, target):
        copy = pltpu.make_async_remote_copy(
            src_ref=src, dst_ref=dst, send_sem=sems.at[0, index], recv_sem=sems.at[1, index],
            device_id=target, device_id_type=MESH,
        )
        copy.start()
        return copy

    sources = sorted(set(range(1, near + 1)) | {near * m for m in range(1, far)} | {windows - 1})
    barrier = pltpu.get_barrier_semaphore()
    for distance in (1, -1):
        pl.semaphore_signal(barrier, inc=1, device_id=at_space(distance), device_id_type=MESH)
    loads = []
    for number, (src, dst) in enumerate([
        (inter_hbm, inter), (state_hbm, state), (neigh_hbm, neigh), (coarse_hbm.at[:, 0, :], coarse),
        (orient_hbm, orient), (deriv_hbm, deriv), (pat_hbm, pat), (jac_hbm.at[:, 0, :], jac), (forcing_hbm, forcing),
    ]):
        if dst is state:
            pair = [(src.at[:, 128 * half : 128 * half + 128], dst.at[half], 9 * half + number) for half in range(2)]
        else:
            pair = [(src, dst, number)]
        loads.append([pltpu.make_async_copy(a, b, in_sem.at[c]) for a, b, c in pair])
        for load in loads[-1]:
            load.start()

    for distance in sources:
        pl.semaphore_signal(barrier, inc=1, device_id=at_tm(-distance), device_id_type=MESH)

    def arrive(number):
        for load in loads[number]:
            load.wait()

    arrive(0)
    for side in range(2):
        hot_inter[side] = one_hot(inter[side : side + 1, :], 0, ELEMS)
    arrive(1)

    def trace_x(values, low):
        return jnp.concatenate([wide(values, slice(64 * f + low, 64 * f + low + 16)) for f in range(FIELDS)], axis=0)

    def halo_start(turn, values):
        right = split(trace_x(values, 48))
        left = split(trace_x(values, 0))
        halo_out[turn, 0] = gathered(right, hot_inter[1])
        halo_out[turn, 1] = gathered(left, hot_inter[0])
        return right, left

    def halo_send(turn):
        return [
            send(halo_out.at[turn, 0], halo_in.at[turn, 0], halo_sem, 2 * turn, at_space(1)),
            send(halo_out.at[turn, 1], halo_in.at[turn, 1], halo_sem, 2 * turn + 1, at_space(-1)),
        ]

    def local_part(values, right, left):
        store_wide(fetched, pl.ds(0, 80), gathered(right, hot[0]))
        store_wide(fetched, pl.ds(160, 80), gathered(left, hot[1]))
        for k in (2, 3):
            low = 8 if k == 2 else 0
            starts = [64 * f + 16 * a + low for f in range(FIELDS) for a in range(4)]
            rows = [wide(values, slice(first, first + 8)) for first in starts]
            store_wide(fetched, pl.ds(160 * k, 160), gathered(split(jnp.concatenate(rows, axis=0)), hot[k]))
        for k in (4, 5):
            low = 3 if k == 4 else 0
            rows = wide(values, pl.ds(low, 80, stride=4))
            store_wide(fetched, pl.ds(160 * k, 80), gathered(split(rows), hot[k]))
        for h in range(FIELDS):
            both = split(wide(values, slice(64 * h, 64 * h + 64)))
            stacked = jnp.concatenate([both, both[:64]], axis=0)
            terms[192 * h : 192 * h + 192, :] = jnp.dot(deriv[...], stacked, preferred_element_type=f32)

    def align(k):
        for half in range(2):
            code = orient[k : k + 1, 128 * half : 128 * half + 128]
            swap, flip_p, flip_q = [jnp.broadcast_to(code & bit, (FIELDS, 128)) != 0 for bit in (4, 2, 1)]
            grid = [[None] * 4 for _ in range(4)]
            for p in range(4):
                for q in range(4):
                    if k in (2, 3):
                        first, stride = 8 * p + (4 if k == 2 else 0) + q, 32
                    else:
                        first, stride = 4 * p + q, 16
                    grid[p][q] = fetched[half, pl.ds(160 * k + first, FIELDS, stride=stride), :]
            grid = [[grid[p][q] if p == q else jnp.where(swap, grid[q][p], grid[p][q]) for q in range(4)] for p in range(4)]
            grid = [[jnp.where(flip_p, grid[3 - p][q], grid[p][q]) for q in range(4)] for p in range(4)]
            grid = [[jnp.where(flip_q, grid[p][3 - q], grid[p][q]) for q in range(4)] for p in range(4)]
            for p in range(4):
                for q in range(4):
                    row = (k // 2 * 64 + face_node(k, p, q)) * 8
                    lifted[half, row : row + FIELDS, :] = (STEP * LIFT) * grid[p][q]

    def halo_part(turn):
        for side, chosen in enumerate((hot_left, hot_right)):
            rows = pl.ds(160 * side, 80)
            total = wide(fetched, rows) + gathered(split(halo_in[turn, side]), chosen[...])
            store_wide(fetched, rows, total)

    def store_middle(row, half, value):
        middle[half, row : row + 32, :] = value

    def store_start(row, half, value):
        start[row : row + 32, 128 * half : 128 * half + 128] = value

    def mix(values, source, store):
        for group in range(2):
            low = 32 * group
            for half in range(2):
                lanes = slice(128 * half, 128 * half + 128)
                own = pat[64 + low : 96 + low, :]
                totals = [
                    own * values[half, 64 * f + low : 64 * f + low + 32, :]
                    + forcing[source, 64 * f + low : 64 * f + low + 32, lanes].astype(f32)
                    for f in range(FIELDS)
                ]
                for d in range(3):
                    sign = pat[128 + 64 * d + low : 160 + 64 * d + low, :]
                    for h in range(FIELDS):
                        face = lifted[half, pl.ds((64 * d + low) * 8 + h, 32, stride=8), :]
                        base = 192 * h + 64 * d + low
                        term = terms[base : base + 32, lanes] + sign * face
                        totals[h] = totals[h] + face
                        for f in range(FIELDS):
                            totals[f] = totals[f] + jac[10 * (5 * d + h) + 2 * f + half : 10 * (5 * d + h) + 2 * f + half + 1, :] * term
                for f in range(FIELDS):
                    store(64 * f + low, half, totals[f])

    def node_sum(piece):
        sums = []
        for f in range(FIELDS):
            halves = [jnp.sum(pat[0:64, :] * piece(64 * f, half), axis=0, keepdims=True) for half in range(2)]
            sums.append(jnp.concatenate(halves, axis=1))
        return jnp.concatenate(sums, axis=0)

    copies = []
    right, left = halo_start(0, state)
    pl.semaphore_wait(barrier, len(sources) + 2)
    halo = halo_send(0)
    lifted[...] = jnp.zeros_like(lifted)
    arrive(3)
    keep = jnp.where(tm == 0, 0.0, 1.0)
    blocks[0] = coarse[...] * keep
    for m in range(1, near):
        copies.append(send(blocks.at[0], blocks.at[m], block_sem, m, at_tm(m)))
    arrive(6)
    ends[...] = node_sum(lambda row, half: state[half, row : row + 64, :])
    end_copy = send(ends, ends_next, end_sem, 0, at_tm(-1))
    arrive(2)
    for k in range(6):
        hot[k] = one_hot(neigh[k : k + 1, :], 0, ELEMS)
    hot_left[...] = one_hot(neigh[0:1, :], ELEMS, SURFACE)
    hot_right[...] = one_hot(neigh[1:2, :], ELEMS + SURFACE, SURFACE)
    arrive(5)
    local_part(state, right, left)
    arrive(4)
    for k in range(2, 6):
        align(k)
    for copy in halo:
        copy.wait()
    halo_part(0)
    align(0)
    align(1)
    arrive(7)
    arrive(8)
    mix(state, 1, store_middle)

    right, left = halo_start(1, middle)
    halo = halo_send(1)
    local_part(middle, right, left)
    for k in range(2, 6):
        align(k)
    for copy in halo:
        copy.wait()
    halo_part(1)
    align(0)
    align(1)
    mix(middle, 0, store_start)

    end_copy.wait()
    coarse_out[...] = node_sum(lambda row, half: start[row : row + 64, 128 * half : 128 * half + 128]) - ends_next[...]
    rounds = [send(coarse_out, coarse_in.at[m], coarse_sem, m, at_tm(m + 1)) for m in range(near)]
    def bulk_send(fields):
        return [
            send(start.at[pl.ds(64 * f, 64)], shifted.at[pl.ds(64 * f, 64)], bulk_sem, f, at_tm(1)) for f in fields
        ]

    bulk = bulk_send(range(EARLY))
    for copy in copies:
        copy.wait()
    columns = [column(blocks.at[near - 1], g) for g in range(5)]
    for m in range(near - 2, -1, -1):
        columns = [matvec(blocks.at[m], vector) for vector in columns]
    for g in range(5):
        for half in range(2):
            products[0, pl.ds(2 * g + half, 5, stride=10), :] = columns[g][:, 128 * half : 128 * half + 128]
    copies = [send(products.at[0], products.at[m], product_sem, m, at_tm(near * m)) for m in range(1, far - 1)]
    for copy in rounds:
        copy.wait()
    vector = coarse_in[near - 1]
    for m in range(near - 2, -1, -1):
        vector = coarse_in[m] + matvec(blocks.at[m], vector)
    window_out[...] = vector
    rounds = [send(window_out, window_in.at[m], window_sem, m, at_tm(near * m)) for m in range(1, far)]
    bulk += bulk_send(range(EARLY, FIELDS))
    for copy in copies:
        copy.wait()
    for copy in rounds:
        copy.wait()
    vector = window_in[far - 1]
    for m in range(far - 2, 0, -1):
        vector = window_in[m] + matvec(products.at[m], vector)
    correction[...] = window_out[...] + matvec(products.at[0], vector)
    for copy in bulk:
        copy.wait()


def solution(mesh):
    windows, parts = mesh.shape["tm"], mesh.shape["space"]
    near = 2 ** ((windows.bit_length() - 1) // 2)
    far = windows // near
    deriv, pattern = tables()
    dma = pltpu.SemaphoreType.DMA

    def per_device(end_state, forcing, jacobians, coarse_blocks, neighbors, orientation, interfaces):
        operands = (
            end_state.reshape(ROWS, ELEMS),
            forcing.reshape(2, ROWS, ELEMS),
            jacobians.reshape(150, 1, 128),
            coarse_blocks.reshape(50, 1, 128),
            neighbors,
            orientation,
            interfaces,
            jnp.asarray(deriv, bf16),
            jnp.asarray(pattern, f32),
        )
        shifted, correction = pl.pallas_call(
            functools.partial(kernel, windows, parts, near, far),
            out_shape=(jax.ShapeDtypeStruct((ROWS, ELEMS), f32), jax.ShapeDtypeStruct((FIELDS, ELEMS), f32)),
            in_specs=[pl.BlockSpec(memory_space=pl.ANY)] * len(operands),
            out_specs=(pl.BlockSpec(memory_space=pl.ANY), pl.BlockSpec(memory_space=pltpu.VMEM)),
            scratch_shapes=[pltpu.VMEM((2, ROWS, 128), f32)]
            + [pltpu.VMEM((x.shape[0], 128) if x.shape[1] == 1 else x.shape, x.dtype) for x in operands[1:]]
            + [
                pltpu.VMEM((6, ELEMS, ELEMS), bf16),
                pltpu.VMEM((SURFACE, ELEMS), bf16),
                pltpu.VMEM((SURFACE, ELEMS), bf16),
                pltpu.VMEM((2, ELEMS, SURFACE), bf16),
                pltpu.VMEM((2, 6 * 160, 128), f32),
                pltpu.VMEM((2, 3 * 64 * 8, 128), f32),
                pltpu.VMEM((15 * 64, ELEMS), f32),
                pltpu.VMEM((2, ROWS, 128), f32),
                pltpu.VMEM((ROWS, ELEMS), f32),
                pltpu.VMEM((2, 2, 80, SURFACE), f32),
                pltpu.VMEM((2, 2, 80, SURFACE), f32),
                pltpu.VMEM((near, 50, 128), f32),
                pltpu.VMEM((max(far - 1, 1), 50, 128), f32),
                pltpu.VMEM((5, ELEMS), f32),
                pltpu.VMEM((5, ELEMS), f32),
                pltpu.VMEM((5, ELEMS), f32),
                pltpu.VMEM((near, 5, ELEMS), f32),
                pltpu.VMEM((5, ELEMS), f32),
                pltpu.VMEM((far, 5, ELEMS), f32),
                dma((18,)),
                dma((2, 4)),
                dma((2, near)),
                dma((2, far)),
                dma((2, 1)),
                dma((2, near)),
                dma((2, far)),
                dma((2, 5)),
            ],
            compiler_params=pltpu.CompilerParams(
                collective_id=0, has_side_effects=True, vmem_limit_bytes=60 * 2**20
            ),
        )(*operands)
        return shifted.reshape(1, FIELDS, NODES, ELEMS) + correction[None, :, None, :]

    in_specs = (
        P("tm", None, None, "space"),
        P("tm", None, None, None, "space"),
        P("tm", None, None, None, "space"),
        P("tm", None, None, "space"),
        P(None, "space"),
        P(None, "space"),
        P(None, "space"),
    )
    out_specs = P("tm", None, None, "space")
    return jax.shard_map(per_device, mesh=mesh, in_specs=in_specs, out_specs=out_specs, check_vma=False)
```

```python
import functools
import math

import jax
import jax.numpy as jnp
import ml_dtypes
import numpy as np
from jax import lax
from jax.experimental import pallas as pl
from jax.experimental.pallas import tpu as pltpu
from jax.sharding import PartitionSpec as P

MESH = pl.DeviceIdType.MESH
FIELDS = 5
NODES = 64
ROWS = FIELDS * NODES
ELEMS = 256
SURFACE = 128
STEP = 0.02
LIFT = 3.0
EARLY = 2
bf16 = jnp.bfloat16
f32 = jnp.float32


def tables():
    x = np.array([-1.0, -math.sqrt(0.2), math.sqrt(0.2), 1.0])
    bary = np.array([1.0 / np.prod([x[j] - x[k] for k in range(4) if k != j]) for j in range(4)])
    d1 = np.zeros((4, 4))
    for i in range(4):
        for j in range(4):
            if i != j:
                d1[i, j] = bary[j] / bary[i] / (x[i] - x[j])
        d1[i, i] = -d1[i].sum()
    eye = np.eye(4)
    derivs = [
        np.kron(np.kron(d1, eye), eye),
        np.kron(np.kron(eye, d1), eye),
        np.kron(np.kron(eye, eye), d1),
    ]
    w1 = np.array([1.0, 5.0, 5.0, 1.0]) / 6.0
    weights = (w1[:, None, None] * w1[None, :, None] * w1[None, None, :]).reshape(64) / 8.0
    n = np.arange(64)
    coords = [n // 16, n // 4 % 4, n % 4]
    blocks = []
    faces = np.zeros(64)
    for d in range(3):
        low, high = coords[d] == 0, coords[d] == 3
        faces += low.astype(float) + high.astype(float)
        blocks.append(STEP * (derivs[d].T + LIFT * np.diag(low.astype(float) - high.astype(float))))
    full = np.concatenate(blocks, axis=0)
    high_part = full.astype(ml_dtypes.bfloat16)
    low_part = (full - high_part.astype(np.float64)).astype(ml_dtypes.bfloat16)
    deriv = np.concatenate([high_part, high_part, low_part], axis=1)
    signs = [np.where(coords[d] == 0, -1.0, 1.0) for d in range(3)]
    own = 1.0 - STEP * LIFT * faces
    pattern = np.stack([weights, own] + signs).astype(np.float32)
    pattern = np.repeat(pattern.reshape(5 * 64, 1), 128, axis=1)
    return deriv, pattern


def face_node(k, p, q):
    if k < 2:
        return 48 * (k & 1) + 4 * p + q
    if k < 4:
        return 16 * p + 12 * (k & 1) + q
    return 16 * p + 4 * q + 3 * (k & 1)


def split(value):
    high = value.astype(bf16)
    low = (value - high.astype(f32)).astype(bf16)
    return jnp.concatenate([high, low], axis=0)


def gathered(both, chosen):
    out = jnp.dot(both, chosen, preferred_element_type=f32)
    half = out.shape[0] // 2
    return out[:half] + out[half:]


def one_hot(index_row, start, count):
    rows = lax.broadcasted_iota(jnp.int32, (count, index_row.shape[1]), 0) + start
    return jnp.where(rows == index_row, 1.0, 0.0).astype(bf16)


def wide(ref, *index):
    return jnp.concatenate([ref[(half, *index, slice(None))] for half in range(2)], axis=1)


def store_wide(ref, index, value):
    for half in range(2):
        ref[half, index, :] = value[:, 128 * half : 128 * half + 128]


def column(block, g):
    return jnp.concatenate([block[pl.ds(2 * g + half, 5, stride=10), :] for half in range(2)], axis=1)


def matvec(block, vector):
    total = column(block, 0) * vector[0:1, :]
    for g in range(1, 5):
        total = total + column(block, g) * vector[g : g + 1, :]
    return total


def kernel(
    windows, parts, near, far,
    state_hbm, forcing_hbm, jac_hbm, coarse_hbm, neigh_hbm, orient_hbm, inter_hbm, deriv_hbm, pat_hbm,
    shifted, correction,
    state, forcing, jac, coarse, neigh, orient, inter, deriv, pat,
    hot, hot_left, hot_right, hot_inter,
    fetched, lifted, terms, middle, start,
    halo_out, halo_in,
    blocks, products, ends, ends_next, coarse_out, coarse_in, window_out, window_in,
    in_sem, halo_sem, block_sem, product_sem, end_sem, coarse_sem, window_sem, bulk_sem,
):
    tm = lax.axis_index("tm")
    space = lax.axis_index("space")
    row, col = lax.div(tm, near), lax.rem(tm, near)

    def at_tm(distance):
        return {"tm": lax.rem(tm + (distance + windows), windows)}

    def at_place(other_row, other_col):
        return {"tm": near * lax.rem(other_row + far, far) + lax.rem(other_col, near)}

    def at_space(distance):
        return {"space": lax.rem(space + (distance + parts), parts)}

    def send(src, dst, sems, index, target):
        copy = pltpu.make_async_remote_copy(
            src_ref=src, dst_ref=dst, send_sem=sems.at[0, index], recv_sem=sems.at[1, index],
            device_id=target, device_id_type=MESH,
        )
        copy.start()
        return copy

    barrier = pltpu.get_barrier_semaphore()
    for distance in (1, -1):
        pl.semaphore_signal(barrier, inc=1, device_id=at_space(distance), device_id_type=MESH)
    loads = []
    for number, (src, dst) in enumerate([
        (inter_hbm, inter), (state_hbm, state), (neigh_hbm, neigh), (coarse_hbm.at[:, 0, :], coarse),
        (orient_hbm, orient), (deriv_hbm, deriv), (pat_hbm, pat), (jac_hbm.at[:, 0, :], jac), (forcing_hbm, forcing),
    ]):
        if dst is state:
            pair = [(src.at[:, 128 * half : 128 * half + 128], dst.at[half], 9 * half + number) for half in range(2)]
        else:
            pair = [(src, dst, number)]
        loads.append([pltpu.make_async_copy(a, b, in_sem.at[c]) for a, b, c in pair])
        for load in loads[-1]:
            load.start()

    targets = [at_place(row, col + m) for m in range(1, near)] + [at_place(row + m, col) for m in range(1, far)]
    last = jnp.where(col == near - 1, 1, 0)
    targets.append(at_place(row - 1 + 2 * last, (near - 1) * (1 - last)))
    for target in targets:
        pl.semaphore_signal(barrier, inc=1, device_id=target, device_id_type=MESH)

    def arrive(number):
        for load in loads[number]:
            load.wait()

    arrive(0)
    for side in range(2):
        hot_inter[side] = one_hot(inter[side : side + 1, :], 0, ELEMS)
    arrive(1)

    def trace_x(values, low):
        return jnp.concatenate([wide(values, slice(64 * f + low, 64 * f + low + 16)) for f in range(FIELDS)], axis=0)

    def halo_start(turn, values):
        right = split(trace_x(values, 48))
        left = split(trace_x(values, 0))
        halo_out[turn, 0] = gathered(right, hot_inter[1])
        halo_out[turn, 1] = gathered(left, hot_inter[0])
        return right, left

    def halo_send(turn):
        return [
            send(halo_out.at[turn, 0], halo_in.at[turn, 0], halo_sem, 2 * turn, at_space(1)),
            send(halo_out.at[turn, 1], halo_in.at[turn, 1], halo_sem, 2 * turn + 1, at_space(-1)),
        ]

    def local_part(values, right, left):
        store_wide(fetched, pl.ds(0, 80), gathered(right, hot[0]))
        store_wide(fetched, pl.ds(160, 80), gathered(left, hot[1]))
        for k in (2, 3):
            low = 8 if k == 2 else 0
            starts = [64 * f + 16 * a + low for f in range(FIELDS) for a in range(4)]
            rows = [wide(values, slice(first, first + 8)) for first in starts]
            store_wide(fetched, pl.ds(160 * k, 160), gathered(split(jnp.concatenate(rows, axis=0)), hot[k]))
        for k in (4, 5):
            low = 3 if k == 4 else 0
            rows = wide(values, pl.ds(low, 80, stride=4))
            store_wide(fetched, pl.ds(160 * k, 80), gathered(split(rows), hot[k]))
        for h in range(FIELDS):
            both = split(wide(values, slice(64 * h, 64 * h + 64)))
            stacked = jnp.concatenate([both, both[:64]], axis=0)
            terms[192 * h : 192 * h + 192, :] = jnp.dot(deriv[...], stacked, preferred_element_type=f32)

    def align(k):
        for half in range(2):
            code = orient[k : k + 1, 128 * half : 128 * half + 128]
            swap, flip_p, flip_q = [jnp.broadcast_to(code & bit, (FIELDS, 128)) != 0 for bit in (4, 2, 1)]
            grid = [[None] * 4 for _ in range(4)]
            for p in range(4):
                for q in range(4):
                    if k in (2, 3):
                        first, stride = 8 * p + (4 if k == 2 else 0) + q, 32
                    else:
                        first, stride = 4 * p + q, 16
                    grid[p][q] = fetched[half, pl.ds(160 * k + first, FIELDS, stride=stride), :]
            grid = [[grid[p][q] if p == q else jnp.where(swap, grid[q][p], grid[p][q]) for q in range(4)] for p in range(4)]
            grid = [[jnp.where(flip_p, grid[3 - p][q], grid[p][q]) for q in range(4)] for p in range(4)]
            grid = [[jnp.where(flip_q, grid[p][3 - q], grid[p][q]) for q in range(4)] for p in range(4)]
            for p in range(4):
                for q in range(4):
                    row = (k // 2 * 64 + face_node(k, p, q)) * 8
                    lifted[half, row : row + FIELDS, :] = (STEP * LIFT) * grid[p][q]

    def halo_part(turn):
        for side, chosen in enumerate((hot_left, hot_right)):
            rows = pl.ds(160 * side, 80)
            total = wide(fetched, rows) + gathered(split(halo_in[turn, side]), chosen[...])
            store_wide(fetched, rows, total)

    def store_middle(row, half, value):
        middle[half, row : row + 32, :] = value

    def store_start(row, half, value):
        start[row : row + 32, 128 * half : 128 * half + 128] = value

    def mix(values, source, store):
        for group in range(2):
            low = 32 * group
            for half in range(2):
                lanes = slice(128 * half, 128 * half + 128)
                own = pat[64 + low : 96 + low, :]
                totals = [
                    own * values[half, 64 * f + low : 64 * f + low + 32, :]
                    + forcing[source, 64 * f + low : 64 * f + low + 32, lanes].astype(f32)
                    for f in range(FIELDS)
                ]
                for d in range(3):
                    sign = pat[128 + 64 * d + low : 160 + 64 * d + low, :]
                    for h in range(FIELDS):
                        face = lifted[half, pl.ds((64 * d + low) * 8 + h, 32, stride=8), :]
                        base = 192 * h + 64 * d + low
                        term = terms[base : base + 32, lanes] + sign * face
                        totals[h] = totals[h] + face
                        for f in range(FIELDS):
                            totals[f] = totals[f] + jac[10 * (5 * d + h) + 2 * f + half : 10 * (5 * d + h) + 2 * f + half + 1, :] * term
                for f in range(FIELDS):
                    store(64 * f + low, half, totals[f])

    def node_sum(piece):
        sums = []
        for f in range(FIELDS):
            halves = [jnp.sum(pat[0:64, :] * piece(64 * f, half), axis=0, keepdims=True) for half in range(2)]
            sums.append(jnp.concatenate(halves, axis=1))
        return jnp.concatenate(sums, axis=0)

    copies = []
    right, left = halo_start(0, state)
    pl.semaphore_wait(barrier, near + far + jnp.where(col == 0, 1, 0) + (near - 1) * last)
    halo = halo_send(0)
    lifted[...] = jnp.zeros_like(lifted)
    arrive(3)
    blocks[pl.ds(col, 1)] = coarse[...][None]
    for m in range(1, near):
        copies.append(send(coarse, blocks.at[col], block_sem, m, at_place(row, col + m)))
    arrive(6)
    ends[...] = node_sum(lambda row, half: state[half, row : row + 64, :])
    end_copy = send(ends, ends_next, end_sem, 0, at_tm(-1))
    arrive(2)
    for k in range(6):
        hot[k] = one_hot(neigh[k : k + 1, :], 0, ELEMS)
    hot_left[...] = one_hot(neigh[0:1, :], ELEMS, SURFACE)
    hot_right[...] = one_hot(neigh[1:2, :], ELEMS + SURFACE, SURFACE)
    arrive(5)
    local_part(state, right, left)
    arrive(4)
    for k in range(2, 6):
        align(k)
    for copy in halo:
        copy.wait()
    halo_part(0)
    align(0)
    align(1)
    arrive(7)
    arrive(8)
    mix(state, 1, store_middle)

    right, left = halo_start(1, middle)
    halo = halo_send(1)
    local_part(middle, right, left)
    for k in range(2, 6):
        align(k)
    for copy in copies:
        copy.wait()
    columns = [column(blocks.at[0], g) for g in range(5)]
    upto = columns
    for m in range(1, near):
        columns = [matvec(blocks.at[m], vector) for vector in columns]
        upto = [jnp.where(col >= m, new, old) for new, old in zip(columns, upto)]
    for slot, matrix in ((0, columns), (far - 1, upto)):
        for g in range(5):
            for half in range(2):
                products[slot, pl.ds(2 * g + half, 5, stride=10), :] = matrix[g][:, 128 * half : 128 * half + 128]
    copies = [
        send(products.at[0], products.at[m], product_sem, m, at_place(row + m, col)) for m in range(1, far - 1)
    ]
    for copy in halo:
        copy.wait()
    halo_part(1)
    align(0)
    align(1)
    mix(middle, 0, store_start)

    end_copy.wait()
    coarse_out[...] = node_sum(lambda row, half: start[row : row + 64, 128 * half : 128 * half + 128]) - ends_next[...]
    slot = lax.rem(col + 1, near)
    rounds = [
        send(coarse_out, coarse_in.at[slot], coarse_sem, m, at_place(row + last, col + 1 + m)) for m in range(near - 1)
    ]
    across = pltpu.make_async_remote_copy(
        src_ref=coarse_out, dst_ref=coarse_in.at[slot], send_sem=coarse_sem.at[0, near - 1],
        recv_sem=coarse_sem.at[1, near - 1], device_id=at_place(row + 1, near - 1), device_id_type=MESH,
    )

    @pl.when(last == 1)
    def _():
        across.start()

    @pl.when(last == 0)
    def _():
        coarse_in[pl.ds(slot, 1)] = coarse_out[...][None]

    def bulk_send(fields):
        return [
            send(start.at[pl.ds(64 * f, 64)], shifted.at[pl.ds(64 * f, 64)], bulk_sem, f, at_tm(1)) for f in fields
        ]

    bulk = bulk_send(range(EARLY))
    for copy in rounds:
        copy.wait()

    @pl.when(last == 1)
    def _():
        across.wait()

    vector = coarse_in[0]
    inside = vector
    for m in range(1, near):
        vector = coarse_in[m] + matvec(blocks.at[m], vector)
        inside = jnp.where(col >= m, vector, inside)
    window_out[...] = vector
    rounds = [send(window_out, window_in.at[m], window_sem, m, at_place(row + m, col)) for m in range(1, far)]
    bulk += bulk_send(range(EARLY, FIELDS))
    for copy in copies:
        copy.wait()
    for copy in rounds:
        copy.wait()
    vector = jnp.where(row >= far - 1, window_in[far - 1], 0.0)
    for m in range(far - 2, 0, -1):
        vector = jnp.where(row >= m, window_in[m] + matvec(products.at[m], vector), 0.0)
    correction[...] = inside + matvec(products.at[far - 1], vector)
    for copy in bulk:
        copy.wait()


def solution(mesh):
    windows, parts = mesh.shape["tm"], mesh.shape["space"]
    near = 2 ** ((windows.bit_length() - 1) // 2)
    far = windows // near
    deriv, pattern = tables()
    dma = pltpu.SemaphoreType.DMA

    def per_device(end_state, forcing, jacobians, coarse_blocks, neighbors, orientation, interfaces):
        operands = (
            end_state.reshape(ROWS, ELEMS),
            forcing.reshape(2, ROWS, ELEMS),
            jacobians.reshape(150, 1, 128),
            coarse_blocks.reshape(50, 1, 128),
            neighbors,
            orientation,
            interfaces,
            jnp.asarray(deriv, bf16),
            jnp.asarray(pattern, f32),
        )
        shifted, correction = pl.pallas_call(
            functools.partial(kernel, windows, parts, near, far),
            out_shape=(jax.ShapeDtypeStruct((ROWS, ELEMS), f32), jax.ShapeDtypeStruct((FIELDS, ELEMS), f32)),
            in_specs=[pl.BlockSpec(memory_space=pl.ANY)] * len(operands),
            out_specs=(pl.BlockSpec(memory_space=pl.ANY), pl.BlockSpec(memory_space=pltpu.VMEM)),
            scratch_shapes=[pltpu.VMEM((2, ROWS, 128), f32)]
            + [pltpu.VMEM((x.shape[0], 128) if x.shape[1] == 1 else x.shape, x.dtype) for x in operands[1:]]
            + [
                pltpu.VMEM((6, ELEMS, ELEMS), bf16),
                pltpu.VMEM((SURFACE, ELEMS), bf16),
                pltpu.VMEM((SURFACE, ELEMS), bf16),
                pltpu.VMEM((2, ELEMS, SURFACE), bf16),
                pltpu.VMEM((2, 6 * 160, 128), f32),
                pltpu.VMEM((2, 3 * 64 * 8, 128), f32),
                pltpu.VMEM((15 * 64, ELEMS), f32),
                pltpu.VMEM((2, ROWS, 128), f32),
                pltpu.VMEM((ROWS, ELEMS), f32),
                pltpu.VMEM((2, 2, 80, SURFACE), f32),
                pltpu.VMEM((2, 2, 80, SURFACE), f32),
                pltpu.VMEM((near, 50, 128), f32),
                pltpu.VMEM((far, 50, 128), f32),
                pltpu.VMEM((5, ELEMS), f32),
                pltpu.VMEM((5, ELEMS), f32),
                pltpu.VMEM((5, ELEMS), f32),
                pltpu.VMEM((near, 5, ELEMS), f32),
                pltpu.VMEM((5, ELEMS), f32),
                pltpu.VMEM((far, 5, ELEMS), f32),
                dma((18,)),
                dma((2, 4)),
                dma((2, near)),
                dma((2, far)),
                dma((2, 1)),
                dma((2, near)),
                dma((2, far)),
                dma((2, 5)),
            ],
            compiler_params=pltpu.CompilerParams(
                collective_id=0, has_side_effects=True, vmem_limit_bytes=60 * 2**20
            ),
        )(*operands)
        return shifted.reshape(1, FIELDS, NODES, ELEMS) + correction[None, :, None, :]

    in_specs = (
        P("tm", None, None, "space"),
        P("tm", None, None, None, "space"),
        P("tm", None, None, None, "space"),
        P("tm", None, None, "space"),
        P(None, "space"),
        P(None, "space"),
        P(None, "space"),
    )
    out_specs = P("tm", None, None, "space")
    return jax.shard_map(per_device, mesh=mesh, in_specs=in_specs, out_specs=out_specs, check_vma=False)
```

```python
import functools
import math

import jax
import jax.numpy as jnp
import ml_dtypes
import numpy as np
from jax import lax
from jax.experimental import pallas as pl
from jax.experimental.pallas import tpu as pltpu
from jax.sharding import PartitionSpec as P

MESH = pl.DeviceIdType.MESH
FIELDS = 5
NODES = 64
ROWS = FIELDS * NODES
ELEMS = 256
SURFACE = 128
STEP = 0.02
LIFT = 3.0
bf16 = jnp.bfloat16
f32 = jnp.float32


def tables():
    x = np.array([-1.0, -math.sqrt(0.2), math.sqrt(0.2), 1.0])
    bary = np.array([1.0 / np.prod([x[j] - x[k] for k in range(4) if k != j]) for j in range(4)])
    d1 = np.zeros((4, 4))
    for i in range(4):
        for j in range(4):
            if i != j:
                d1[i, j] = bary[j] / bary[i] / (x[i] - x[j])
        d1[i, i] = -d1[i].sum()
    eye = np.eye(4)
    derivs = [
        np.kron(np.kron(d1, eye), eye),
        np.kron(np.kron(eye, d1), eye),
        np.kron(np.kron(eye, eye), d1),
    ]
    w1 = np.array([1.0, 5.0, 5.0, 1.0]) / 6.0
    weights = (w1[:, None, None] * w1[None, :, None] * w1[None, None, :]).reshape(64) / 8.0
    n = np.arange(64)
    coords = [n // 16, n // 4 % 4, n % 4]
    blocks = []
    faces = np.zeros(64)
    for d in range(3):
        low, high = coords[d] == 0, coords[d] == 3
        faces += low.astype(float) + high.astype(float)
        blocks.append(STEP * (derivs[d].T + LIFT * np.diag(low.astype(float) - high.astype(float))))
    full = np.concatenate(blocks, axis=0)
    high_part = full.astype(ml_dtypes.bfloat16)
    low_part = (full - high_part.astype(np.float64)).astype(ml_dtypes.bfloat16)
    deriv = np.concatenate([high_part, high_part, low_part], axis=1)
    signs = [np.where(coords[d] == 0, -1.0, 1.0) for d in range(3)]
    own = 1.0 - STEP * LIFT * faces
    pattern = np.stack([weights, own] + signs).astype(np.float32)
    pattern = np.repeat(pattern.reshape(5 * 64, 1), 128, axis=1)
    return deriv, pattern


def face_node(k, p, q):
    if k < 2:
        return 48 * (k & 1) + 4 * p + q
    if k < 4:
        return 16 * p + 12 * (k & 1) + q
    return 16 * p + 4 * q + 3 * (k & 1)


def split(value):
    high = value.astype(bf16)
    low = (value - high.astype(f32)).astype(bf16)
    return jnp.concatenate([high, low], axis=0)


def gathered(both, chosen):
    out = jnp.dot(both, chosen, preferred_element_type=f32)
    half = out.shape[0] // 2
    return out[:half] + out[half:]


def one_hot(index_row, start, count):
    rows = lax.broadcasted_iota(jnp.int32, (count, index_row.shape[1]), 0) + start
    return jnp.where(rows == index_row, 1.0, 0.0).astype(bf16)


def wide(ref, *index):
    return jnp.concatenate([ref[(half, *index, slice(None))] for half in range(2)], axis=1)


def store_wide(ref, index, value):
    for half in range(2):
        ref[half, index, :] = value[:, 128 * half : 128 * half + 128]


def column(block, g):
    return jnp.concatenate([block[pl.ds(2 * g + half, 5, stride=10), :] for half in range(2)], axis=1)


def matvec(block, vector):
    total = column(block, 0) * vector[0:1, :]
    for g in range(1, 5):
        total = total + column(block, g) * vector[g : g + 1, :]
    return total


def kernel(
    windows, parts, near, far,
    state_hbm, forcing_hbm, jac_hbm, coarse_hbm, neigh_hbm, orient_hbm, inter_hbm, deriv_hbm, pat_hbm,
    shifted, correction,
    state, forcing, jac, coarse, neigh, orient, inter, deriv, pat,
    hot, hot_left, hot_right, hot_inter,
    fetched, lifted, terms, middle, start,
    halo_out, halo_in,
    blocks, products, ends, ends_next, coarse_out, coarse_in, window_out, window_in,
    in_sem, halo_sem, block_sem, product_sem, end_sem, coarse_sem, window_sem, bulk_sem,
):
    tm = lax.axis_index("tm")
    space = lax.axis_index("space")
    row, col = lax.div(tm, near), lax.rem(tm, near)

    def at_tm(distance):
        return {"tm": lax.rem(tm + (distance + windows), windows)}

    def at_place(other_row, other_col):
        return {"tm": near * lax.rem(other_row + far, far) + lax.rem(other_col, near)}

    def at_space(distance):
        return {"space": lax.rem(space + (distance + parts), parts)}

    def send(src, dst, sems, index, target):
        copy = pltpu.make_async_remote_copy(
            src_ref=src, dst_ref=dst, send_sem=sems.at[0, index], recv_sem=sems.at[1, index],
            device_id=target, device_id_type=MESH,
        )
        copy.start()
        return copy

    barrier = pltpu.get_barrier_semaphore()
    for distance in (1, -1):
        pl.semaphore_signal(barrier, inc=1, device_id=at_space(distance), device_id_type=MESH)
    loads = []
    for number, (src, dst) in enumerate([
        (inter_hbm, inter), (state_hbm, state), (neigh_hbm, neigh), (coarse_hbm.at[:, 0, :], coarse),
        (orient_hbm, orient), (deriv_hbm, deriv), (pat_hbm, pat), (jac_hbm.at[:, 0, :], jac), (forcing_hbm, forcing),
    ]):
        if dst is state:
            pair = [(src.at[:, 128 * half : 128 * half + 128], dst.at[half], 9 * half + number) for half in range(2)]
        else:
            pair = [(src, dst, number)]
        loads.append([pltpu.make_async_copy(a, b, in_sem.at[c]) for a, b, c in pair])
        for load in loads[-1]:
            load.start()

    targets = [at_place(row, col + m) for m in range(1, near)] + [at_place(row + m, col) for m in range(1, far)]
    last = jnp.where(col == near - 1, 1, 0)
    targets.append(at_place(row - 1 + 2 * last, (near - 1) * (1 - last)))
    for target in targets:
        pl.semaphore_signal(barrier, inc=1, device_id=target, device_id_type=MESH)

    def arrive(number):
        for load in loads[number]:
            load.wait()

    arrive(0)
    for side in range(2):
        hot_inter[side] = one_hot(inter[side : side + 1, :], 0, ELEMS)
    arrive(1)

    def trace_x(values, low):
        return jnp.concatenate([wide(values, slice(64 * f + low, 64 * f + low + 16)) for f in range(FIELDS)], axis=0)

    def halo_start(turn, values):
        right = split(trace_x(values, 48))
        left = split(trace_x(values, 0))
        halo_out[turn, 0] = gathered(right, hot_inter[1])
        halo_out[turn, 1] = gathered(left, hot_inter[0])
        return right, left

    def halo_send(turn):
        return [
            send(halo_out.at[turn, 0], halo_in.at[turn, 0], halo_sem, 2 * turn, at_space(1)),
            send(halo_out.at[turn, 1], halo_in.at[turn, 1], halo_sem, 2 * turn + 1, at_space(-1)),
        ]

    def local_part(values, right, left):
        store_wide(fetched, pl.ds(0, 80), gathered(right, hot[0]))
        store_wide(fetched, pl.ds(160, 80), gathered(left, hot[1]))
        for k in (2, 3):
            low = 8 if k == 2 else 0
            starts = [64 * f + 16 * a + low for f in range(FIELDS) for a in range(4)]
            rows = [wide(values, slice(first, first + 8)) for first in starts]
            store_wide(fetched, pl.ds(160 * k, 160), gathered(split(jnp.concatenate(rows, axis=0)), hot[k]))
        for k in (4, 5):
            low = 3 if k == 4 else 0
            rows = wide(values, pl.ds(low, 80, stride=4))
            store_wide(fetched, pl.ds(160 * k, 80), gathered(split(rows), hot[k]))
        for h in range(FIELDS):
            both = split(wide(values, slice(64 * h, 64 * h + 64)))
            stacked = jnp.concatenate([both, both[:64]], axis=0)
            terms[192 * h : 192 * h + 192, :] = jnp.dot(deriv[...], stacked, preferred_element_type=f32)

    def align(k):
        for half in range(2):
            code = orient[k : k + 1, 128 * half : 128 * half + 128]
            swap, flip_p, flip_q = [jnp.broadcast_to(code & bit, (FIELDS, 128)) != 0 for bit in (4, 2, 1)]
            grid = [[None] * 4 for _ in range(4)]
            for p in range(4):
                for q in range(4):
                    if k in (2, 3):
                        first, stride = 8 * p + (4 if k == 2 else 0) + q, 32
                    else:
                        first, stride = 4 * p + q, 16
                    grid[p][q] = fetched[half, pl.ds(160 * k + first, FIELDS, stride=stride), :]
            grid = [[grid[p][q] if p == q else jnp.where(swap, grid[q][p], grid[p][q]) for q in range(4)] for p in range(4)]
            grid = [[jnp.where(flip_p, grid[3 - p][q], grid[p][q]) for q in range(4)] for p in range(4)]
            grid = [[jnp.where(flip_q, grid[p][3 - q], grid[p][q]) for q in range(4)] for p in range(4)]
            for p in range(4):
                for q in range(4):
                    row = (k // 2 * 64 + face_node(k, p, q)) * 8
                    lifted[half, row : row + FIELDS, :] = (STEP * LIFT) * grid[p][q]

    def halo_part(turn):
        for side, chosen in enumerate((hot_left, hot_right)):
            rows = pl.ds(160 * side, 80)
            total = wide(fetched, rows) + gathered(split(halo_in[turn, side]), chosen[...])
            store_wide(fetched, rows, total)

    def store_middle(field, low, count, half, value):
        middle[half, 64 * field + low : 64 * field + low + count, :] = value

    def store_start(field, low, count, half, value):
        start[field, low : low + count, 128 * half : 128 * half + 128] = value

    def mix(values, source, store, low, count):
        for half in range(2):
            lanes = slice(128 * half, 128 * half + 128)
            own = pat[64 + low : 64 + low + count, :]
            totals = [
                own * values[half, 64 * f + low : 64 * f + low + count, :]
                + forcing[source, 64 * f + low : 64 * f + low + count, lanes].astype(f32)
                for f in range(FIELDS)
            ]
            for d in range(3):
                sign = pat[128 + 64 * d + low : 128 + 64 * d + low + count, :]
                for h in range(FIELDS):
                    base = 192 * h + 64 * d + low
                    term = terms[base : base + count, lanes]
                    if d > 0 or low in (0, 48):
                        face = lifted[half, pl.ds((64 * d + low) * 8 + h, count, stride=8), :]
                        term = term + sign * face
                        totals[h] = totals[h] + face
                    for f in range(FIELDS):
                        number = 10 * (5 * d + h) + 2 * f + half
                        totals[f] = totals[f] + jac[number : number + 1, :] * term
            for f in range(FIELDS):
                store(f, low, count, half, totals[f])

    def inner(values, source, store):
        mix(values, source, store, 16, 32)

    def outer(values, source, store):
        mix(values, source, store, 0, 16)
        mix(values, source, store, 48, 16)

    def node_sum(piece, low, count):
        sums = []
        for f in range(FIELDS):
            halves = [
                jnp.sum(pat[low : low + count, :] * piece(f, low, count, half), axis=0, keepdims=True)
                for half in range(2)
            ]
            sums.append(jnp.concatenate(halves, axis=1))
        return jnp.concatenate(sums, axis=0)

    def state_piece(f, low, count, half):
        return state[half, 64 * f + low : 64 * f + low + count, :]

    def start_piece(f, low, count, half):
        return start[f, low : low + count, 128 * half : 128 * half + 128]

    def bulk_send(index, low, count):
        rows = pl.ds(low, count)
        return send(start.at[:, rows], shifted.at[:, rows], bulk_sem, index, at_tm(1))

    copies = []
    right, left = halo_start(0, state)
    pl.semaphore_wait(barrier, near + far + jnp.where(col == 0, 1, 0) + (near - 1) * last)
    halo = halo_send(0)
    lifted[...] = jnp.zeros_like(lifted)
    arrive(3)
    blocks[pl.ds(col, 1)] = coarse[...][None]
    for m in range(1, near):
        copies.append(send(coarse, blocks.at[col], block_sem, m, at_place(row, col + m)))
    arrive(6)
    ends[...] = node_sum(state_piece, 0, 64)
    end_copy = send(ends, ends_next, end_sem, 0, at_tm(-1))
    arrive(2)
    for k in range(6):
        hot[k] = one_hot(neigh[k : k + 1, :], 0, ELEMS)
    hot_left[...] = one_hot(neigh[0:1, :], ELEMS, SURFACE)
    hot_right[...] = one_hot(neigh[1:2, :], ELEMS + SURFACE, SURFACE)
    arrive(5)
    local_part(state, right, left)
    arrive(4)
    for k in range(2, 6):
        align(k)
    arrive(7)
    arrive(8)
    inner(state, 1, store_middle)
    for copy in halo:
        copy.wait()
    halo_part(0)
    align(0)
    align(1)
    outer(state, 1, store_middle)

    right, left = halo_start(1, middle)
    halo = halo_send(1)
    local_part(middle, right, left)
    for k in range(2, 6):
        align(k)
    inner(middle, 0, store_start)
    bulk = [bulk_send(0, 16, 32)]
    end_copy.wait()
    coarse_out[...] = node_sum(start_piece, 16, 32) - ends_next[...]
    for copy in copies:
        copy.wait()
    columns = [column(blocks.at[0], g) for g in range(5)]
    upto = columns
    for m in range(1, near):
        columns = [matvec(blocks.at[m], vector) for vector in columns]
        upto = [jnp.where(col >= m, new, old) for new, old in zip(columns, upto)]
    for slot, matrix in ((0, columns), (far - 1, upto)):
        for g in range(5):
            for half in range(2):
                products[slot, pl.ds(2 * g + half, 5, stride=10), :] = matrix[g][:, 128 * half : 128 * half + 128]
    copies = [
        send(products.at[0], products.at[m], product_sem, m, at_place(row + m, col)) for m in range(1, far - 1)
    ]
    for copy in halo:
        copy.wait()
    halo_part(1)
    align(0)
    align(1)
    outer(middle, 0, store_start)
    coarse_out[...] = coarse_out[...] + node_sum(start_piece, 0, 16) + node_sum(start_piece, 48, 16)
    slot = lax.rem(col + 1, near)
    rounds = [
        send(coarse_out, coarse_in.at[slot], coarse_sem, m, at_place(row + last, col + 1 + m)) for m in range(near - 1)
    ]
    across = pltpu.make_async_remote_copy(
        src_ref=coarse_out, dst_ref=coarse_in.at[slot], send_sem=coarse_sem.at[0, near - 1],
        recv_sem=coarse_sem.at[1, near - 1], device_id=at_place(row + 1, near - 1), device_id_type=MESH,
    )

    @pl.when(last == 1)
    def _():
        across.start()

    @pl.when(last == 0)
    def _():
        coarse_in[pl.ds(slot, 1)] = coarse_out[...][None]

    bulk += [bulk_send(1, 0, 16), bulk_send(2, 48, 16)]
    for copy in rounds:
        copy.wait()

    @pl.when(last == 1)
    def _():
        across.wait()

    vector = coarse_in[0]
    inside = vector
    for m in range(1, near):
        vector = coarse_in[m] + matvec(blocks.at[m], vector)
        inside = jnp.where(col >= m, vector, inside)
    window_out[...] = vector
    rounds = [send(window_out, window_in.at[m], window_sem, m, at_place(row + m, col)) for m in range(1, far)]
    for copy in copies:
        copy.wait()
    for copy in rounds:
        copy.wait()
    vector = jnp.where(row >= far - 1, window_in[far - 1], 0.0)
    for m in range(far - 2, 0, -1):
        vector = jnp.where(row >= m, window_in[m] + matvec(products.at[m], vector), 0.0)
    correction[...] = inside + matvec(products.at[far - 1], vector)
    for copy in bulk:
        copy.wait()


def solution(mesh):
    windows, parts = mesh.shape["tm"], mesh.shape["space"]
    near = 2 ** ((windows.bit_length() - 1) // 2)
    far = windows // near
    deriv, pattern = tables()
    dma = pltpu.SemaphoreType.DMA

    def per_device(end_state, forcing, jacobians, coarse_blocks, neighbors, orientation, interfaces):
        operands = (
            end_state.reshape(ROWS, ELEMS),
            forcing.reshape(2, ROWS, ELEMS),
            jacobians.reshape(150, 1, 128),
            coarse_blocks.reshape(50, 1, 128),
            neighbors,
            orientation,
            interfaces,
            jnp.asarray(deriv, bf16),
            jnp.asarray(pattern, f32),
        )
        shifted, correction = pl.pallas_call(
            functools.partial(kernel, windows, parts, near, far),
            out_shape=(pltpu.VMEM((FIELDS, NODES, ELEMS), f32), pltpu.VMEM((FIELDS, ELEMS), f32)),
            in_specs=[pl.BlockSpec(memory_space=pl.ANY)] * len(operands),
            out_specs=(pl.BlockSpec(memory_space=pltpu.VMEM), pl.BlockSpec(memory_space=pltpu.VMEM)),
            scratch_shapes=[pltpu.VMEM((2, ROWS, 128), f32)]
            + [pltpu.VMEM((x.shape[0], 128) if x.shape[1] == 1 else x.shape, x.dtype) for x in operands[1:]]
            + [
                pltpu.VMEM((6, ELEMS, ELEMS), bf16),
                pltpu.VMEM((SURFACE, ELEMS), bf16),
                pltpu.VMEM((SURFACE, ELEMS), bf16),
                pltpu.VMEM((2, ELEMS, SURFACE), bf16),
                pltpu.VMEM((2, 6 * 160, 128), f32),
                pltpu.VMEM((2, 3 * 64 * 8, 128), f32),
                pltpu.VMEM((15 * 64, ELEMS), f32),
                pltpu.VMEM((2, ROWS, 128), f32),
                pltpu.VMEM((FIELDS, NODES, ELEMS), f32),
                pltpu.VMEM((2, 2, 80, SURFACE), f32),
                pltpu.VMEM((2, 2, 80, SURFACE), f32),
                pltpu.VMEM((near, 50, 128), f32),
                pltpu.VMEM((far, 50, 128), f32),
                pltpu.VMEM((5, ELEMS), f32),
                pltpu.VMEM((5, ELEMS), f32),
                pltpu.VMEM((5, ELEMS), f32),
                pltpu.VMEM((near, 5, ELEMS), f32),
                pltpu.VMEM((5, ELEMS), f32),
                pltpu.VMEM((far, 5, ELEMS), f32),
                dma((18,)),
                dma((2, 4)),
                dma((2, near)),
                dma((2, far)),
                dma((2, 1)),
                dma((2, near)),
                dma((2, far)),
                dma((2, 3)),
            ],
            compiler_params=pltpu.CompilerParams(
                collective_id=0, has_side_effects=True, vmem_limit_bytes=60 * 2**20
            ),
        )(*operands)
        return shifted[None] + correction[None, :, None, :]

    in_specs = (
        P("tm", None, None, "space"),
        P("tm", None, None, None, "space"),
        P("tm", None, None, None, "space"),
        P("tm", None, None, "space"),
        P(None, "space"),
        P(None, "space"),
        P(None, "space"),
    )
    out_specs = P("tm", None, None, "space")
    return jax.shard_map(per_device, mesh=mesh, in_specs=in_specs, out_specs=out_specs, check_vma=False)
```

```python
import functools
import math

import jax
import jax.numpy as jnp
import ml_dtypes
import numpy as np
from jax import lax
from jax.experimental import pallas as pl
from jax.experimental.pallas import tpu as pltpu
from jax.sharding import PartitionSpec as P

MESH = pl.DeviceIdType.MESH
FIELDS = 5
NODES = 64
ROWS = FIELDS * NODES
ELEMS = 256
SURFACE = 128
STEP = 0.02
LIFT = 3.0
bf16 = jnp.bfloat16
f32 = jnp.float32


def tables():
    x = np.array([-1.0, -math.sqrt(0.2), math.sqrt(0.2), 1.0])
    bary = np.array([1.0 / np.prod([x[j] - x[k] for k in range(4) if k != j]) for j in range(4)])
    d1 = np.zeros((4, 4))
    for i in range(4):
        for j in range(4):
            if i != j:
                d1[i, j] = bary[j] / bary[i] / (x[i] - x[j])
        d1[i, i] = -d1[i].sum()
    eye = np.eye(4)
    derivs = [
        np.kron(np.kron(d1, eye), eye),
        np.kron(np.kron(eye, d1), eye),
        np.kron(np.kron(eye, eye), d1),
    ]
    w1 = np.array([1.0, 5.0, 5.0, 1.0]) / 6.0
    weights = (w1[:, None, None] * w1[None, :, None] * w1[None, None, :]).reshape(64) / 8.0
    n = np.arange(64)
    coords = [n // 16, n // 4 % 4, n % 4]
    blocks = []
    faces = np.zeros(64)
    for d in range(3):
        low, high = coords[d] == 0, coords[d] == 3
        faces += low.astype(float) + high.astype(float)
        blocks.append(STEP * (derivs[d].T + LIFT * np.diag(low.astype(float) - high.astype(float))))
    full = np.concatenate(blocks, axis=0)
    high_part = full.astype(ml_dtypes.bfloat16)
    low_part = (full - high_part.astype(np.float64)).astype(ml_dtypes.bfloat16)
    deriv = np.concatenate([high_part, high_part, low_part], axis=1)
    signs = [np.where(coords[d] == 0, -1.0, 1.0) for d in range(3)]
    own = 1.0 - STEP * LIFT * faces
    pattern = np.stack([weights, own] + signs).astype(np.float32)
    pattern = np.repeat(pattern.reshape(5 * 64, 1), 128, axis=1)
    return deriv, pattern


def face_node(k, p, q):
    if k < 2:
        return 48 * (k & 1) + 4 * p + q
    if k < 4:
        return 16 * p + 12 * (k & 1) + q
    return 16 * p + 4 * q + 3 * (k & 1)


def split(value):
    high = value.astype(bf16)
    low = (value - high.astype(f32)).astype(bf16)
    return jnp.concatenate([high, low], axis=0)


def gathered(both, chosen):
    out = jnp.dot(both, chosen, preferred_element_type=f32)
    half = out.shape[0] // 2
    return out[:half] + out[half:]


def one_hot(index_row, start, count):
    rows = lax.broadcasted_iota(jnp.int32, (count, index_row.shape[1]), 0) + start
    return jnp.where(rows == index_row, 1.0, 0.0).astype(bf16)


def wide(ref, *index):
    return jnp.concatenate([ref[(half, *index, slice(None))] for half in range(2)], axis=1)


def store_wide(ref, index, value):
    for half in range(2):
        ref[half, index, :] = value[:, 128 * half : 128 * half + 128]


def column(block, g):
    return jnp.concatenate([block[pl.ds(2 * g + half, 5, stride=10), :] for half in range(2)], axis=1)


def matvec(block, vector):
    total = column(block, 0) * vector[0:1, :]
    for g in range(1, 5):
        total = total + column(block, g) * vector[g : g + 1, :]
    return total


def kernel(
    windows, parts, near, far,
    state_hbm, forcing_hbm, jac_hbm, coarse_hbm, neigh_hbm, orient_hbm, inter_hbm, deriv_hbm, pat_hbm,
    shifted, correction,
    state, forcing, jac, coarse, neigh, orient, inter, deriv, pat,
    hot, hot_left, hot_right, hot_inter,
    fetched, lifted, terms, middle, start,
    halo_out, halo_in,
    blocks, products, ends, ends_next, coarse_out, coarse_in, window_out, window_in,
    in_sem, halo_sem, block_sem, product_sem, end_sem, coarse_sem, window_sem, bulk_sem,
):
    tm = lax.axis_index("tm")
    space = lax.axis_index("space")
    row, col = lax.div(tm, near), lax.rem(tm, near)

    def at_tm(distance):
        return {"tm": lax.rem(tm + (distance + windows), windows)}

    def at_place(other_row, other_col):
        return {"tm": near * lax.rem(other_row + far, far) + lax.rem(other_col, near)}

    def at_space(distance):
        return {"space": lax.rem(space + (distance + parts), parts)}

    def send(src, dst, sems, index, target):
        copy = pltpu.make_async_remote_copy(
            src_ref=src, dst_ref=dst, send_sem=sems.at[0, index], recv_sem=sems.at[1, index],
            device_id=target, device_id_type=MESH,
        )
        copy.start()
        return copy

    barrier = pltpu.get_barrier_semaphore()
    for distance in (1, -1):
        pl.semaphore_signal(barrier, inc=1, device_id=at_space(distance), device_id_type=MESH)
    def down_copy(src, dst, sems, m):
        return pltpu.make_async_remote_copy(
            src_ref=src, dst_ref=dst, send_sem=sems.at[0, m], recv_sem=sems.at[1, m],
            device_id=at_place(row + m, col), device_id_type=MESH,
        )

    def down(src, dst, sems, m):
        @pl.when(row + m < far)
        def _():
            down_copy(src, dst, sems, m).start()

    def down_wait(src, dst, sems, m):
        @pl.when(row + m < far)
        def _():
            down_copy(src, dst, sems, m).wait_send()

        @pl.when(row >= m)
        def _():
            down_copy(src, dst, sems, m).wait_recv()

    loads = []
    for number, (src, dst) in enumerate([
        (inter_hbm, inter), (state_hbm, state), (neigh_hbm, neigh), (coarse_hbm.at[:, 0, :], coarse),
        (orient_hbm, orient), (deriv_hbm, deriv), (pat_hbm, pat), (jac_hbm.at[:, 0, :], jac), (forcing_hbm, forcing),
    ]):
        if dst is state:
            pair = [(src.at[:, 128 * half : 128 * half + 128], dst.at[half], 9 * half + number) for half in range(2)]
        else:
            pair = [(src, dst, number)]
        loads.append([pltpu.make_async_copy(a, b, in_sem.at[c]) for a, b, c in pair])
        for load in loads[-1]:
            load.start()

    targets = [at_place(row, col + m) for m in range(1, near)] + [at_place(row + m, col) for m in range(1, far)]
    last = jnp.where(col == near - 1, 1, 0)
    targets.append(at_place(row - 1 + 2 * last, (near - 1) * (1 - last)))
    for target in targets:
        pl.semaphore_signal(barrier, inc=1, device_id=target, device_id_type=MESH)

    def arrive(number):
        for load in loads[number]:
            load.wait()

    arrive(0)
    for side in range(2):
        hot_inter[side] = one_hot(inter[side : side + 1, :], 0, ELEMS)
    arrive(1)

    def trace_x(values, low):
        return jnp.concatenate([wide(values, slice(64 * f + low, 64 * f + low + 16)) for f in range(FIELDS)], axis=0)

    def halo_start(turn, values):
        right = split(trace_x(values, 48))
        left = split(trace_x(values, 0))
        halo_out[turn, 0] = gathered(right, hot_inter[1])
        halo_out[turn, 1] = gathered(left, hot_inter[0])
        return right, left

    def halo_send(turn):
        return [
            send(halo_out.at[turn, 0], halo_in.at[turn, 0], halo_sem, 2 * turn, at_space(1)),
            send(halo_out.at[turn, 1], halo_in.at[turn, 1], halo_sem, 2 * turn + 1, at_space(-1)),
        ]

    def local_part(values, right, left):
        store_wide(fetched, pl.ds(0, 80), gathered(right, hot[0]))
        store_wide(fetched, pl.ds(160, 80), gathered(left, hot[1]))
        for k in (2, 3):
            low = 8 if k == 2 else 0
            starts = [64 * f + 16 * a + low for f in range(FIELDS) for a in range(4)]
            rows = [wide(values, slice(first, first + 8)) for first in starts]
            store_wide(fetched, pl.ds(160 * k, 160), gathered(split(jnp.concatenate(rows, axis=0)), hot[k]))
        for k in (4, 5):
            low = 3 if k == 4 else 0
            rows = wide(values, pl.ds(low, 80, stride=4))
            store_wide(fetched, pl.ds(160 * k, 80), gathered(split(rows), hot[k]))
        for h in range(FIELDS):
            both = split(wide(values, slice(64 * h, 64 * h + 64)))
            stacked = jnp.concatenate([both, both[:64]], axis=0)
            terms[192 * h : 192 * h + 192, :] = jnp.dot(deriv[...], stacked, preferred_element_type=f32)

    def align(k):
        for half in range(2):
            code = orient[k : k + 1, 128 * half : 128 * half + 128]
            swap, flip_p, flip_q = [jnp.broadcast_to(code & bit, (FIELDS, 128)) != 0 for bit in (4, 2, 1)]
            grid = [[None] * 4 for _ in range(4)]
            for p in range(4):
                for q in range(4):
                    if k in (2, 3):
                        first, stride = 8 * p + (4 if k == 2 else 0) + q, 32
                    else:
                        first, stride = 4 * p + q, 16
                    grid[p][q] = fetched[half, pl.ds(160 * k + first, FIELDS, stride=stride), :]
            grid = [[grid[p][q] if p == q else jnp.where(swap, grid[q][p], grid[p][q]) for q in range(4)] for p in range(4)]
            grid = [[jnp.where(flip_p, grid[3 - p][q], grid[p][q]) for q in range(4)] for p in range(4)]
            grid = [[jnp.where(flip_q, grid[p][3 - q], grid[p][q]) for q in range(4)] for p in range(4)]
            for p in range(4):
                for q in range(4):
                    row = (k // 2 * 64 + face_node(k, p, q)) * 8
                    lifted[half, row : row + FIELDS, :] = (STEP * LIFT) * grid[p][q]

    def halo_part(turn):
        for side, chosen in enumerate((hot_left, hot_right)):
            rows = pl.ds(160 * side, 80)
            total = wide(fetched, rows) + gathered(split(halo_in[turn, side]), chosen[...])
            store_wide(fetched, rows, total)

    def store_middle(field, low, count, half, value):
        middle[half, 64 * field + low : 64 * field + low + count, :] = value

    def store_start(field, low, count, half, value):
        start[field, low : low + count, 128 * half : 128 * half + 128] = value

    def mix(values, source, store, low, count):
        for half in range(2):
            lanes = slice(128 * half, 128 * half + 128)
            own = pat[64 + low : 64 + low + count, :]
            totals = [
                own * values[half, 64 * f + low : 64 * f + low + count, :]
                + forcing[source, 64 * f + low : 64 * f + low + count, lanes].astype(f32)
                for f in range(FIELDS)
            ]
            for d in range(3):
                sign = pat[128 + 64 * d + low : 128 + 64 * d + low + count, :]
                for h in range(FIELDS):
                    base = 192 * h + 64 * d + low
                    term = terms[base : base + count, lanes]
                    if d > 0 or low in (0, 48):
                        face = lifted[half, pl.ds((64 * d + low) * 8 + h, count, stride=8), :]
                        term = term + sign * face
                        totals[h] = totals[h] + face
                    for f in range(FIELDS):
                        number = 10 * (5 * d + h) + 2 * f + half
                        totals[f] = totals[f] + jac[number : number + 1, :] * term
            for f in range(FIELDS):
                store(f, low, count, half, totals[f])

    def inner(values, source, store):
        mix(values, source, store, 16, 32)

    def outer(values, source, store):
        mix(values, source, store, 0, 16)
        mix(values, source, store, 48, 16)

    def node_sum(piece, low, count):
        sums = []
        for f in range(FIELDS):
            halves = [
                jnp.sum(pat[low : low + count, :] * piece(f, low, count, half), axis=0, keepdims=True)
                for half in range(2)
            ]
            sums.append(jnp.concatenate(halves, axis=1))
        return jnp.concatenate(sums, axis=0)

    def state_piece(f, low, count, half):
        return state[half, 64 * f + low : 64 * f + low + count, :]

    def start_piece(f, low, count, half):
        return start[f, low : low + count, 128 * half : 128 * half + 128]

    def bulk_send(index, low, count):
        rows = pl.ds(low, count)
        return send(start.at[:, rows], shifted.at[:, rows], bulk_sem, index, at_tm(1))

    copies = []
    right, left = halo_start(0, state)
    pl.semaphore_wait(barrier, near + far + jnp.where(col == 0, 1, 0) + (near - 1) * last)
    halo = halo_send(0)
    lifted[...] = jnp.zeros_like(lifted)
    arrive(3)
    blocks[pl.ds(col, 1)] = coarse[...][None]
    for m in range(1, near):
        copies.append(send(coarse, blocks.at[col], block_sem, m, at_place(row, col + m)))
    arrive(6)
    ends[...] = node_sum(state_piece, 0, 64)
    end_copy = send(ends, ends_next, end_sem, 0, at_tm(-1))
    arrive(2)
    for k in range(6):
        hot[k] = one_hot(neigh[k : k + 1, :], 0, ELEMS)
    hot_left[...] = one_hot(neigh[0:1, :], ELEMS, SURFACE)
    hot_right[...] = one_hot(neigh[1:2, :], ELEMS + SURFACE, SURFACE)
    arrive(5)
    local_part(state, right, left)
    arrive(4)
    for k in range(2, 6):
        align(k)
    arrive(7)
    arrive(8)
    inner(state, 1, store_middle)
    for copy in halo:
        copy.wait()
    halo_part(0)
    align(0)
    align(1)
    outer(state, 1, store_middle)

    right, left = halo_start(1, middle)
    halo = halo_send(1)
    local_part(middle, right, left)
    for k in range(2, 6):
        align(k)
    inner(middle, 0, store_start)
    bulk = [bulk_send(0, 16, 32)]
    end_copy.wait()
    coarse_out[...] = node_sum(start_piece, 16, 32) - ends_next[...]
    for copy in copies:
        copy.wait()
    columns = [column(blocks.at[0], g) for g in range(5)]
    upto = columns
    for m in range(1, near):
        columns = [matvec(blocks.at[m], vector) for vector in columns]
        upto = [jnp.where(col >= m, new, old) for new, old in zip(columns, upto)]
    for slot, matrix in ((0, columns), (far - 1, upto)):
        for g in range(5):
            for half in range(2):
                products[slot, pl.ds(2 * g + half, 5, stride=10), :] = matrix[g][:, 128 * half : 128 * half + 128]
    for m in range(1, far - 1):
        down(products.at[0], products.at[m], product_sem, m)

        @pl.when(row < m)
        def _():
            products[m] = jnp.zeros((50, 128), f32)

    for m in range(1, far):

        @pl.when(row < m)
        def _():
            window_in[m] = jnp.zeros((FIELDS, ELEMS), f32)

    for copy in halo:
        copy.wait()
    halo_part(1)
    align(0)
    align(1)
    outer(middle, 0, store_start)
    coarse_out[...] = coarse_out[...] + node_sum(start_piece, 0, 16) + node_sum(start_piece, 48, 16)
    slot = lax.rem(col + 1, near)
    rounds = [
        send(coarse_out, coarse_in.at[slot], coarse_sem, m, at_place(row + last, col + 1 + m)) for m in range(near - 1)
    ]
    across = pltpu.make_async_remote_copy(
        src_ref=coarse_out, dst_ref=coarse_in.at[slot], send_sem=coarse_sem.at[0, near - 1],
        recv_sem=coarse_sem.at[1, near - 1], device_id=at_place(row + 1, near - 1), device_id_type=MESH,
    )

    @pl.when(last == 1)
    def _():
        across.start()

    @pl.when(last == 0)
    def _():
        coarse_in[pl.ds(slot, 1)] = coarse_out[...][None]

    bulk += [bulk_send(1, 0, 16), bulk_send(2, 48, 16)]
    for copy in rounds:
        copy.wait()

    @pl.when(last == 1)
    def _():
        across.wait()

    vector = coarse_in[0]
    inside = vector
    for m in range(1, near):
        vector = coarse_in[m] + matvec(blocks.at[m], vector)
        inside = jnp.where(col >= m, vector, inside)
    window_out[...] = vector
    for m in range(1, far):
        down(window_out, window_in.at[m], window_sem, m)
    for m in range(1, far - 1):
        down_wait(products.at[0], products.at[m], product_sem, m)
    for m in range(1, far):
        down_wait(window_out, window_in.at[m], window_sem, m)
    vector = window_in[far - 1]
    for m in range(far - 2, 0, -1):
        vector = window_in[m] + matvec(products.at[m], vector)
    correction[...] = inside + matvec(products.at[far - 1], vector)
    for copy in bulk:
        copy.wait()


def solution(mesh):
    windows, parts = mesh.shape["tm"], mesh.shape["space"]
    near = 2 ** ((windows.bit_length() - 1) // 2)
    far = windows // near
    deriv, pattern = tables()
    dma = pltpu.SemaphoreType.DMA

    def per_device(end_state, forcing, jacobians, coarse_blocks, neighbors, orientation, interfaces):
        operands = (
            end_state.reshape(ROWS, ELEMS),
            forcing.reshape(2, ROWS, ELEMS),
            jacobians.reshape(150, 1, 128),
            coarse_blocks.reshape(50, 1, 128),
            neighbors,
            orientation,
            interfaces,
            jnp.asarray(deriv, bf16),
            jnp.asarray(pattern, f32),
        )
        shifted, correction = pl.pallas_call(
            functools.partial(kernel, windows, parts, near, far),
            out_shape=(pltpu.VMEM((FIELDS, NODES, ELEMS), f32), pltpu.VMEM((FIELDS, ELEMS), f32)),
            in_specs=[pl.BlockSpec(memory_space=pl.ANY)] * len(operands),
            out_specs=(pl.BlockSpec(memory_space=pltpu.VMEM), pl.BlockSpec(memory_space=pltpu.VMEM)),
            scratch_shapes=[pltpu.VMEM((2, ROWS, 128), f32)]
            + [pltpu.VMEM((x.shape[0], 128) if x.shape[1] == 1 else x.shape, x.dtype) for x in operands[1:]]
            + [
                pltpu.VMEM((6, ELEMS, ELEMS), bf16),
                pltpu.VMEM((SURFACE, ELEMS), bf16),
                pltpu.VMEM((SURFACE, ELEMS), bf16),
                pltpu.VMEM((2, ELEMS, SURFACE), bf16),
                pltpu.VMEM((2, 6 * 160, 128), f32),
                pltpu.VMEM((2, 3 * 64 * 8, 128), f32),
                pltpu.VMEM((15 * 64, ELEMS), f32),
                pltpu.VMEM((2, ROWS, 128), f32),
                pltpu.VMEM((FIELDS, NODES, ELEMS), f32),
                pltpu.VMEM((2, 2, 80, SURFACE), f32),
                pltpu.VMEM((2, 2, 80, SURFACE), f32),
                pltpu.VMEM((near, 50, 128), f32),
                pltpu.VMEM((far, 50, 128), f32),
                pltpu.VMEM((5, ELEMS), f32),
                pltpu.VMEM((5, ELEMS), f32),
                pltpu.VMEM((5, ELEMS), f32),
                pltpu.VMEM((near, 5, ELEMS), f32),
                pltpu.VMEM((5, ELEMS), f32),
                pltpu.VMEM((far, 5, ELEMS), f32),
                dma((18,)),
                dma((2, 4)),
                dma((2, near)),
                dma((2, far)),
                dma((2, 1)),
                dma((2, near)),
                dma((2, far)),
                dma((2, 3)),
            ],
            compiler_params=pltpu.CompilerParams(
                collective_id=0, has_side_effects=True, vmem_limit_bytes=60 * 2**20
            ),
        )(*operands)
        return shifted[None] + correction[None, :, None, :]

    in_specs = (
        P("tm", None, None, "space"),
        P("tm", None, None, None, "space"),
        P("tm", None, None, None, "space"),
        P("tm", None, None, "space"),
        P(None, "space"),
        P(None, "space"),
        P(None, "space"),
    )
    out_specs = P("tm", None, None, "space")
    return jax.shard_map(per_device, mesh=mesh, in_specs=in_specs, out_specs=out_specs, check_vma=False)
```

```python
import functools
import math

import jax
import jax.numpy as jnp
import ml_dtypes
import numpy as np
from jax import lax
from jax.experimental import pallas as pl
from jax.experimental.pallas import tpu as pltpu
from jax.sharding import PartitionSpec as P

MESH = pl.DeviceIdType.MESH
FIELDS = 5
NODES = 64
ROWS = FIELDS * NODES
ELEMS = 256
SURFACE = 128
STEP = 0.02
LIFT = 3.0
bf16 = jnp.bfloat16
f32 = jnp.float32


def tables():
    x = np.array([-1.0, -math.sqrt(0.2), math.sqrt(0.2), 1.0])
    bary = np.array([1.0 / np.prod([x[j] - x[k] for k in range(4) if k != j]) for j in range(4)])
    d1 = np.zeros((4, 4))
    for i in range(4):
        for j in range(4):
            if i != j:
                d1[i, j] = bary[j] / bary[i] / (x[i] - x[j])
        d1[i, i] = -d1[i].sum()
    eye = np.eye(4)
    derivs = [
        np.kron(np.kron(d1, eye), eye),
        np.kron(np.kron(eye, d1), eye),
        np.kron(np.kron(eye, eye), d1),
    ]
    w1 = np.array([1.0, 5.0, 5.0, 1.0]) / 6.0
    weights = (w1[:, None, None] * w1[None, :, None] * w1[None, None, :]).reshape(64) / 8.0
    n = np.arange(64)
    coords = [n // 16, n // 4 % 4, n % 4]
    blocks = []
    faces = np.zeros(64)
    for d in range(3):
        low, high = coords[d] == 0, coords[d] == 3
        faces += low.astype(float) + high.astype(float)
        blocks.append(STEP * (derivs[d].T + LIFT * np.diag(low.astype(float) - high.astype(float))))
    full = np.concatenate(blocks, axis=0)
    high_part = full.astype(ml_dtypes.bfloat16)
    low_part = (full - high_part.astype(np.float64)).astype(ml_dtypes.bfloat16)
    deriv = np.concatenate([high_part, high_part, low_part], axis=1)
    signs = [np.where(coords[d] == 0, -1.0, 1.0) for d in range(3)]
    own = 1.0 - STEP * LIFT * faces
    pattern = np.stack([weights, own] + signs).astype(np.float32)
    pattern = np.repeat(pattern.reshape(5 * 64, 1), 128, axis=1)
    return deriv, pattern


def face_node(k, p, q):
    if k < 2:
        return 48 * (k & 1) + 4 * p + q
    if k < 4:
        return 16 * p + 12 * (k & 1) + q
    return 16 * p + 4 * q + 3 * (k & 1)


def split(value):
    high = value.astype(bf16)
    low = (value - high.astype(f32)).astype(bf16)
    return jnp.concatenate([high, low], axis=0)


def gathered(both, chosen):
    out = jnp.dot(both, chosen, preferred_element_type=f32)
    half = out.shape[0] // 2
    return out[:half] + out[half:]


def one_hot(index_row, start, count):
    rows = lax.broadcasted_iota(jnp.int32, (count, index_row.shape[1]), 0) + start
    return jnp.where(rows == index_row, 1.0, 0.0).astype(bf16)


def wide(ref, *index):
    return jnp.concatenate([ref[(half, *index, slice(None))] for half in range(2)], axis=1)


def store_wide(ref, index, value):
    for half in range(2):
        ref[half, index, :] = value[:, 128 * half : 128 * half + 128]


def column(block, g):
    return jnp.concatenate([block[pl.ds(2 * g + half, 5, stride=10), :] for half in range(2)], axis=1)


def matvec(block, vector):
    total = column(block, 0) * vector[0:1, :]
    for g in range(1, 5):
        total = total + column(block, g) * vector[g : g + 1, :]
    return total


def kernel(
    windows, parts, near, far,
    state_hbm, forcing_hbm, jac_hbm, coarse_hbm, neigh_hbm, orient_hbm, inter_hbm, deriv_hbm, pat_hbm,
    shifted, correction,
    state, forcing, jac, coarse, neigh, orient, inter, deriv, pat,
    hot, hot_left, hot_right, hot_inter,
    fetched, lifted, terms, middle, start,
    halo_out, halo_in,
    blocks, products, ends, ends_next, coarse_out, coarse_in, window_out, window_in,
    in_sem, halo_sem, block_sem, product_sem, end_sem, coarse_sem, window_sem, bulk_sem,
):
    tm = lax.axis_index("tm")
    space = lax.axis_index("space")
    row, col = lax.div(tm, near), lax.rem(tm, near)

    def at_tm(distance):
        return {"tm": lax.rem(tm + (distance + windows), windows)}

    def at_place(other_row, other_col):
        return {"tm": near * lax.rem(other_row + far, far) + lax.rem(other_col, near)}

    def at_space(distance):
        return {"space": lax.rem(space + (distance + parts), parts)}

    def send(src, dst, sems, index, target):
        copy = pltpu.make_async_remote_copy(
            src_ref=src, dst_ref=dst, send_sem=sems.at[0, index], recv_sem=sems.at[1, index],
            device_id=target, device_id_type=MESH,
        )
        copy.start()
        return copy

    barrier = pltpu.get_barrier_semaphore()
    for distance in (1, -1):
        pl.semaphore_signal(barrier, inc=1, device_id=at_space(distance), device_id_type=MESH)
    def down_copy(src, dst, sems, m):
        return pltpu.make_async_remote_copy(
            src_ref=src, dst_ref=dst, send_sem=sems.at[0, m], recv_sem=sems.at[1, m],
            device_id=at_place(row + m, col), device_id_type=MESH,
        )

    def down(src, dst, sems, m, first=0):
        @pl.when((row >= first) & (row + m < far))
        def _():
            down_copy(src, dst, sems, m).start()

    def down_wait(src, dst, sems, m, first=0):
        @pl.when((row >= first) & (row + m < far))
        def _():
            down_copy(src, dst, sems, m).wait_send()

        @pl.when(row >= m + first)
        def _():
            down_copy(src, dst, sems, m).wait_recv()

    loads = []
    for number, (src, dst) in enumerate([
        (inter_hbm, inter), (state_hbm, state), (neigh_hbm, neigh), (coarse_hbm.at[:, 0, :], coarse),
        (orient_hbm, orient), (deriv_hbm, deriv), (pat_hbm, pat), (jac_hbm.at[:, 0, :], jac), (forcing_hbm, forcing),
    ]):
        if dst is state:
            pair = [(src.at[:, 128 * half : 128 * half + 128], dst.at[half], 9 * half + number) for half in range(2)]
        else:
            pair = [(src, dst, number)]
        loads.append([pltpu.make_async_copy(a, b, in_sem.at[c]) for a, b, c in pair])
        for load in loads[-1]:
            load.start()

    targets = [at_place(row, col + m) for m in range(1, near)] + [at_place(row + m, col) for m in range(1, far)]
    last = jnp.where(col == near - 1, 1, 0)
    targets.append(at_place(row - 1 + 2 * last, (near - 1) * (1 - last)))
    for target in targets:
        pl.semaphore_signal(barrier, inc=1, device_id=target, device_id_type=MESH)

    def arrive(number):
        for load in loads[number]:
            load.wait()

    arrive(0)
    for side in range(2):
        hot_inter[side] = one_hot(inter[side : side + 1, :], 0, ELEMS)
    arrive(1)

    def trace_x(values, low):
        return jnp.concatenate([wide(values, slice(64 * f + low, 64 * f + low + 16)) for f in range(FIELDS)], axis=0)

    def halo_start(turn, values):
        right = split(trace_x(values, 48))
        left = split(trace_x(values, 0))
        halo_out[turn, 0] = gathered(right, hot_inter[1])
        halo_out[turn, 1] = gathered(left, hot_inter[0])
        return right, left

    def halo_send(turn):
        return [
            send(halo_out.at[turn, 0], halo_in.at[turn, 0], halo_sem, 2 * turn, at_space(1)),
            send(halo_out.at[turn, 1], halo_in.at[turn, 1], halo_sem, 2 * turn + 1, at_space(-1)),
        ]

    def local_x(right, left):
        store_wide(fetched, pl.ds(0, 80), gathered(right, hot[0]))
        store_wide(fetched, pl.ds(160, 80), gathered(left, hot[1]))

    def local_part(values):
        for k in (2, 3):
            low = 8 if k == 2 else 0
            starts = [64 * f + 16 * a + low for f in range(FIELDS) for a in range(4)]
            rows = [wide(values, slice(first, first + 8)) for first in starts]
            store_wide(fetched, pl.ds(160 * k, 160), gathered(split(jnp.concatenate(rows, axis=0)), hot[k]))
        for k in (4, 5):
            low = 3 if k == 4 else 0
            rows = wide(values, pl.ds(low, 80, stride=4))
            store_wide(fetched, pl.ds(160 * k, 80), gathered(split(rows), hot[k]))
        for h in range(FIELDS):
            both = split(wide(values, slice(64 * h, 64 * h + 64)))
            stacked = jnp.concatenate([both, both[:64]], axis=0)
            terms[192 * h : 192 * h + 192, :] = jnp.dot(deriv[...], stacked, preferred_element_type=f32)

    def align(k):
        for half in range(2):
            code = orient[k : k + 1, 128 * half : 128 * half + 128]
            swap, flip_p, flip_q = [jnp.broadcast_to(code & bit, (FIELDS, 128)) != 0 for bit in (4, 2, 1)]
            grid = [[None] * 4 for _ in range(4)]
            for p in range(4):
                for q in range(4):
                    if k in (2, 3):
                        first, stride = 8 * p + (4 if k == 2 else 0) + q, 32
                    else:
                        first, stride = 4 * p + q, 16
                    grid[p][q] = fetched[half, pl.ds(160 * k + first, FIELDS, stride=stride), :]
            grid = [[grid[p][q] if p == q else jnp.where(swap, grid[q][p], grid[p][q]) for q in range(4)] for p in range(4)]
            grid = [[jnp.where(flip_p, grid[3 - p][q], grid[p][q]) for q in range(4)] for p in range(4)]
            grid = [[jnp.where(flip_q, grid[p][3 - q], grid[p][q]) for q in range(4)] for p in range(4)]
            for p in range(4):
                for q in range(4):
                    row = (k // 2 * 64 + face_node(k, p, q)) * 8
                    lifted[half, row : row + FIELDS, :] = (STEP * LIFT) * grid[p][q]

    def halo_part(turn):
        for side, chosen in enumerate((hot_left, hot_right)):
            rows = pl.ds(160 * side, 80)
            total = wide(fetched, rows) + gathered(split(halo_in[turn, side]), chosen[...])
            store_wide(fetched, rows, total)

    def store_middle(field, low, count, half, value):
        middle[half, 64 * field + low : 64 * field + low + count, :] = value

    def store_start(field, low, count, half, value):
        start[field, low : low + count, 128 * half : 128 * half + 128] = value

    def mix(values, source, store, low, count):
        for half in range(2):
            lanes = slice(128 * half, 128 * half + 128)
            own = pat[64 + low : 64 + low + count, :]
            totals = [
                own * values[half, 64 * f + low : 64 * f + low + count, :]
                + forcing[source, 64 * f + low : 64 * f + low + count, lanes].astype(f32)
                for f in range(FIELDS)
            ]
            for d in range(3):
                sign = pat[128 + 64 * d + low : 128 + 64 * d + low + count, :]
                for h in range(FIELDS):
                    base = 192 * h + 64 * d + low
                    term = terms[base : base + count, lanes]
                    if d > 0 or low in (0, 48):
                        face = lifted[half, pl.ds((64 * d + low) * 8 + h, count, stride=8), :]
                        term = term + sign * face
                        totals[h] = totals[h] + face
                    for f in range(FIELDS):
                        number = 10 * (5 * d + h) + 2 * f + half
                        totals[f] = totals[f] + jac[number : number + 1, :] * term
            for f in range(FIELDS):
                store(f, low, count, half, totals[f])

    def inner(values, source, store):
        mix(values, source, store, 16, 32)

    def outer(values, source, store):
        mix(values, source, store, 0, 16)
        mix(values, source, store, 48, 16)

    def node_sum(piece, low, count):
        sums = []
        for f in range(FIELDS):
            halves = [
                jnp.sum(pat[low : low + count, :] * piece(f, low, count, half), axis=0, keepdims=True)
                for half in range(2)
            ]
            sums.append(jnp.concatenate(halves, axis=1))
        return jnp.concatenate(sums, axis=0)

    def state_piece(f, low, count, half):
        return state[half, 64 * f + low : 64 * f + low + count, :]

    def start_piece(f, low, count, half):
        return start[f, low : low + count, 128 * half : 128 * half + 128]

    def bulk_send(index, low, count):
        rows = pl.ds(low, count)
        return send(start.at[:, rows], shifted.at[:, rows], bulk_sem, index, at_tm(1))

    copies = []
    right, left = halo_start(0, state)
    pl.semaphore_wait(barrier, near + far + jnp.where(col == 0, 1, 0) + (near - 1) * last)
    halo = halo_send(0)
    lifted[...] = jnp.zeros_like(lifted)
    arrive(3)
    blocks[pl.ds(col, 1)] = coarse[...][None]
    for m in range(1, near):
        copies.append(send(coarse, blocks.at[col], block_sem, m, at_place(row, col + m)))
    arrive(6)
    ends[...] = node_sum(state_piece, 0, 64)
    end_copy = send(ends, ends_next, end_sem, 0, at_tm(-1))
    arrive(2)
    for k in range(6):
        hot[k] = one_hot(neigh[k : k + 1, :], 0, ELEMS)
    hot_left[...] = one_hot(neigh[0:1, :], ELEMS, SURFACE)
    hot_right[...] = one_hot(neigh[1:2, :], ELEMS + SURFACE, SURFACE)
    arrive(5)
    local_part(state)
    arrive(4)
    for k in range(2, 6):
        align(k)
    arrive(7)
    arrive(8)
    inner(state, 1, store_middle)
    local_x(right, left)
    for copy in halo:
        copy.wait()
    halo_part(0)
    align(0)
    align(1)
    outer(state, 1, store_middle)

    right, left = halo_start(1, middle)
    halo = halo_send(1)
    local_part(middle)
    for k in range(2, 6):
        align(k)
    inner(middle, 0, store_start)
    bulk = [bulk_send(0, 16, 32)]
    local_x(right, left)
    end_copy.wait()
    coarse_out[...] = node_sum(start_piece, 16, 32) - ends_next[...]
    for copy in copies:
        copy.wait()
    columns = [column(blocks.at[0], g) for g in range(5)]
    upto = columns
    for m in range(1, near):
        columns = [matvec(blocks.at[m], vector) for vector in columns]
        upto = [jnp.where(col >= m, new, old) for new, old in zip(columns, upto)]
    for slot, matrix in ((0, columns), (far - 1, upto)):
        for g in range(5):
            for half in range(2):
                products[slot, pl.ds(2 * g + half, 5, stride=10), :] = matrix[g][:, 128 * half : 128 * half + 128]
    for m in range(1, far - 1):
        down(products.at[0], products.at[m], product_sem, m, 1)

        @pl.when(row < m + 1)
        def _():
            products[m] = jnp.zeros((50, 128), f32)

    for m in range(1, far):

        @pl.when(row < m)
        def _():
            window_in[m] = jnp.zeros((FIELDS, ELEMS), f32)

    for copy in halo:
        copy.wait()
    halo_part(1)
    align(0)
    align(1)
    outer(middle, 0, store_start)
    coarse_out[...] = coarse_out[...] + node_sum(start_piece, 0, 16) + node_sum(start_piece, 48, 16)
    slot = lax.rem(col + 1, near)
    rounds = [
        send(coarse_out, coarse_in.at[slot], coarse_sem, m, at_place(row + last, col + 1 + m)) for m in range(near - 1)
    ]
    across = pltpu.make_async_remote_copy(
        src_ref=coarse_out, dst_ref=coarse_in.at[slot], send_sem=coarse_sem.at[0, near - 1],
        recv_sem=coarse_sem.at[1, near - 1], device_id=at_place(row + 1, near - 1), device_id_type=MESH,
    )

    @pl.when(last == 1)
    def _():
        across.start()

    @pl.when(last == 0)
    def _():
        coarse_in[pl.ds(slot, 1)] = coarse_out[...][None]

    bulk += [bulk_send(1, 0, 16), bulk_send(2, 48, 16)]
    for copy in rounds:
        copy.wait()

    @pl.when(last == 1)
    def _():
        across.wait()

    vector = coarse_in[0]
    inside = vector
    for m in range(1, near):
        vector = coarse_in[m] + matvec(blocks.at[m], vector)
        inside = jnp.where(col >= m, vector, inside)
    window_out[...] = vector
    for m in range(1, far):
        down(window_out, window_in.at[m], window_sem, m)
    for m in range(1, far - 1):
        down_wait(products.at[0], products.at[m], product_sem, m, 1)
    for m in range(1, far):
        down_wait(window_out, window_in.at[m], window_sem, m)
    vector = window_in[far - 1]
    for m in range(far - 2, 0, -1):
        vector = window_in[m] + matvec(products.at[m], vector)
    correction[...] = inside + matvec(products.at[far - 1], vector)
    for copy in bulk:
        copy.wait()


def solution(mesh):
    windows, parts = mesh.shape["tm"], mesh.shape["space"]
    near = 2 ** ((windows.bit_length() - 1) // 2)
    far = windows // near
    deriv, pattern = tables()
    dma = pltpu.SemaphoreType.DMA

    def per_device(end_state, forcing, jacobians, coarse_blocks, neighbors, orientation, interfaces):
        operands = (
            end_state.reshape(ROWS, ELEMS),
            forcing.reshape(2, ROWS, ELEMS),
            jacobians.reshape(150, 1, 128),
            coarse_blocks.reshape(50, 1, 128),
            neighbors,
            orientation,
            interfaces,
            jnp.asarray(deriv, bf16),
            jnp.asarray(pattern, f32),
        )
        shifted, correction = pl.pallas_call(
            functools.partial(kernel, windows, parts, near, far),
            out_shape=(pltpu.VMEM((FIELDS, NODES, ELEMS), f32), pltpu.VMEM((FIELDS, ELEMS), f32)),
            in_specs=[pl.BlockSpec(memory_space=pl.ANY)] * len(operands),
            out_specs=(pl.BlockSpec(memory_space=pltpu.VMEM), pl.BlockSpec(memory_space=pltpu.VMEM)),
            scratch_shapes=[pltpu.VMEM((2, ROWS, 128), f32)]
            + [pltpu.VMEM((x.shape[0], 128) if x.shape[1] == 1 else x.shape, x.dtype) for x in operands[1:]]
            + [
                pltpu.VMEM((6, ELEMS, ELEMS), bf16),
                pltpu.VMEM((SURFACE, ELEMS), bf16),
                pltpu.VMEM((SURFACE, ELEMS), bf16),
                pltpu.VMEM((2, ELEMS, SURFACE), bf16),
                pltpu.VMEM((2, 6 * 160, 128), f32),
                pltpu.VMEM((2, 3 * 64 * 8, 128), f32),
                pltpu.VMEM((15 * 64, ELEMS), f32),
                pltpu.VMEM((2, ROWS, 128), f32),
                pltpu.VMEM((FIELDS, NODES, ELEMS), f32),
                pltpu.VMEM((2, 2, 80, SURFACE), f32),
                pltpu.VMEM((2, 2, 80, SURFACE), f32),
                pltpu.VMEM((near, 50, 128), f32),
                pltpu.VMEM((far, 50, 128), f32),
                pltpu.VMEM((5, ELEMS), f32),
                pltpu.VMEM((5, ELEMS), f32),
                pltpu.VMEM((5, ELEMS), f32),
                pltpu.VMEM((near, 5, ELEMS), f32),
                pltpu.VMEM((5, ELEMS), f32),
                pltpu.VMEM((far, 5, ELEMS), f32),
                dma((18,)),
                dma((2, 4)),
                dma((2, near)),
                dma((2, far)),
                dma((2, 1)),
                dma((2, near)),
                dma((2, far)),
                dma((2, 3)),
            ],
            compiler_params=pltpu.CompilerParams(
                collective_id=0, has_side_effects=True, vmem_limit_bytes=60 * 2**20
            ),
        )(*operands)
        return shifted[None] + correction[None, :, None, :]

    in_specs = (
        P("tm", None, None, "space"),
        P("tm", None, None, None, "space"),
        P("tm", None, None, None, "space"),
        P("tm", None, None, "space"),
        P(None, "space"),
        P(None, "space"),
        P(None, "space"),
    )
    out_specs = P("tm", None, None, "space")
    return jax.shard_map(per_device, mesh=mesh, in_specs=in_specs, out_specs=out_specs, check_vma=False)
```
